32 devices in a mesh: group: 2 (over x), seq: 8 (over z, y), tp: 2 (over core).
Axes of the slice: x: 2, y: 2, z: 4, core: 2. Of those that a mesh axis runs over, the one named last changes fastest.
Arguments:
- queries: bfloat16 [2048, 2048], P(('group', 'seq'), 'tp'), parts along dimension 0, may hold values from -32 to 32
- keys: bfloat16 [16384, 2048], P(('group', 'seq'), 'tp'), parts along dimension 0, may hold values from -14 to 14
- values: bfloat16 [16384, 2048], P(('group', 'seq'), 'tp'), parts along dimension 0, may hold values from -6 to 6
- out_grad: bfloat16 [2048, 2048], P(('group', 'seq', 'tp')), parts along dimension 0, may hold values from -6 to 6
- starts: int32 [32], P('group'), parts along dimension 0, may hold values from 0 to 7168, as said below
Outputs:
- grad_queries: bfloat16 [2048, 2048], P(('group', 'seq'), 'tp'), parts along dimension 0
- grad_keys: bfloat16 [16384, 2048], P(('group', 'seq'), 'tp'), parts along dimension 0
- grad_values: bfloat16 [16384, 2048], P(('group', 'seq'), 'tp'), parts along dimension 0
The draws below stay inside these ranges and needn't reach their ends.
There are 2 independent parts, one for each index of `group`. The reference program is written for one: setup_inputs(seed, part) draws one part's arguments, and reference() takes and returns one part's arrays. A program takes and returns all parts, laid end to end along the dimension named above; each array names one. Nothing has to cross between parts.
Inputs may be any that keep to these rules, and one draw needn't show every extreme that they name: Each entry is a multiple of 64. For block b with d = b // 2, starts[b] lies between max(0, (d - 1) * 1024) and min((d + 1) * 1024, 7168); the first block of each d takes the lower of these ends and the last block of each d the upper one.
All inputs are finite; a program needn't handle non-finite values.
Results may differ from the reference program's by a relative error of at most 0.015.
Values may be sent and summed in bfloat16 or wider, within the bound.
No kernel may reach another device: no remote copies, remote signals or barrier semaphores. Data moves between devices by JAX's collectives and lax.ppermute only.
A program may use at most 192 MiB of HBM per device.

```python
import math
import jax
import jax.numpy as jnp
from jax import lax

HEADS = 16
HD = 128
WIN = 1024
BLK = 64
EV_DEV = 1024
BPD = 2
FRAMES = 1024
EVENTS = 8192
NBLK = 16


def window_starts(key):
    block_ids = jnp.arange(NBLK, dtype=jnp.int32)
    owner = block_ids // BPD
    position = block_ids % BPD
    lowest = jnp.maximum(0, (owner - 1) * EV_DEV)
    highest = jnp.minimum((owner + 1) * EV_DEV, EVENTS - WIN)
    spread_count = (highest - lowest) // BLK + 1
    drawn = jax.random.randint(jax.random.fold_in(key, 11), (NBLK,), 0, 1 << 20)
    picked = lowest + BLK * (drawn % spread_count)
    picked = jnp.where(position == 0, lowest, picked)
    picked = jnp.where(position == BPD - 1, highest, picked)
    return picked.astype(jnp.int32)


def base_keys(key):
    return jnp.clip(jax.random.normal(jax.random.fold_in(key, 12), (EVENTS, HEADS * HD), jnp.float32), -4.5, 4.5)


def draw_starts(key, part):
    return window_starts(key)


def draw_keys(key, part):
    base = base_keys(key)
    return base.astype(jnp.bfloat16)


def draw_queries(key, part):
    base = jnp.clip(jax.random.normal(jax.random.fold_in(key, 14), (FRAMES, HEADS * HD), jnp.float32), -4.5, 4.5)
    return base.astype(jnp.bfloat16)


def block_levels(own_key, extent, cuts, low, largest):
    def one(axis_at, shards_of):
        draws = jax.random.uniform(jax.random.fold_in(jax.random.fold_in(own_key, 6), axis_at), (shards_of,), jnp.float32, low / len(cuts), largest / len(cuts))
        return jnp.repeat(jnp.exp(draws), extent[axis_at] // shards_of).reshape((-1,) + (1,) * (len(extent) - axis_at - 1))

    factor_of = one(*cuts[0])
    for cut in cuts[1:]:
        factor_of = factor_of * one(*cut)
    return factor_of


def centred(rng, dims, spread, most, shards=(), held_as=jnp.bfloat16):
    entries = spread * jax.random.normal(rng, dims, jnp.float32)
    if shards:
        entries = entries * block_levels(rng, dims, shards, -0.22, 0.18)
    return jnp.clip(entries, -most, most).astype(held_as)


def setup_inputs(seed: int = 0, part: int = 0) -> dict:
    streams_of = jax.random.split(jax.random.key(seed), 6)
    part_splits = jax.random.split(jax.random.fold_in(streams_of[5], part), 6)
    return {
        "queries": draw_queries(jax.random.fold_in(jax.random.fold_in(streams_of[5], part), 71), part),
        "keys": draw_keys(jax.random.fold_in(jax.random.fold_in(streams_of[5], part), 71), part),
        "values": centred(part_splits[2], (EVENTS, HEADS * HD), 1.0, 6.0, ((0, 8), (1, 2))),
        "out_grad": centred(part_splits[3], (FRAMES, HEADS * HD), 1.0, 6.0, ((0, 16),)),
        "starts": draw_starts(jax.random.fold_in(jax.random.fold_in(streams_of[5], part), 71), part),
    }


def reference(queries, keys, values, out_grad, starts):
    width = queries.shape[1]
    heads = width // HD
    scale = 1.0 / math.sqrt(HD)
    q_blocks = queries.reshape(NBLK, BLK, heads, HD)
    g_blocks = out_grad.reshape(NBLK, BLK, heads, HD)

    def step(carry, item):
        acc_k, acc_v = carry
        q_blk, g_blk, begin = item
        q32 = q_blk.astype(jnp.float32)
        g32 = g_blk.astype(jnp.float32)
        key_win = lax.dynamic_slice_in_dim(keys, begin, WIN).reshape(WIN, heads, HD).astype(jnp.float32)
        val_win = lax.dynamic_slice_in_dim(values, begin, WIN).reshape(WIN, heads, HD).astype(jnp.float32)
        scores = jnp.einsum('qhd,khd->hqk', q32, key_win) * scale
        top = lax.optimization_barrier(jnp.max(scores, axis=-1, keepdims=True))
        lse = top + jnp.log(lax.optimization_barrier(jnp.sum(jnp.exp(scores - top), axis=-1, keepdims=True)))
        probs = jnp.exp(scores - lse)
        probs_low = lax.optimization_barrier(probs.astype(jnp.bfloat16))
        p32 = probs_low.astype(jnp.float32)
        attended = jnp.einsum('hqk,khd->qhd', p32, val_win)
        delta = lax.optimization_barrier(jnp.sum(g32 * attended, axis=-1)).T
        dprobs = jnp.einsum('qhd,khd->hqk', g32, val_win)
        dscores = lax.optimization_barrier((scale * probs * (dprobs - delta[:, :, None])).astype(jnp.bfloat16))
        d32 = dscores.astype(jnp.float32)
        grad_q = jnp.einsum('hqk,khd->qhd', d32, key_win).reshape(BLK, width)
        grad_k = jnp.einsum('hqk,qhd->khd', d32, q32).reshape(WIN, width)
        grad_v = jnp.einsum('hqk,qhd->khd', p32, g32).reshape(WIN, width)
        acc_k = lax.dynamic_update_slice_in_dim(acc_k, lax.dynamic_slice_in_dim(acc_k, begin, WIN) + grad_k, begin, 0)
        acc_v = lax.dynamic_update_slice_in_dim(acc_v, lax.dynamic_slice_in_dim(acc_v, begin, WIN) + grad_v, begin, 0)
        return ((acc_k, acc_v), grad_q.astype(jnp.bfloat16))
    zeros = jnp.zeros((EVENTS, width), jnp.float32)
    (acc_k, acc_v), grad_q = lax.scan(step, (zeros, zeros), (q_blocks, g_blocks, starts.astype(jnp.int32)))
    return (grad_q.reshape(FRAMES, width), acc_k.astype(jnp.bfloat16), acc_v.astype(jnp.bfloat16))
```

```python
import functools
import math

import jax
import jax.numpy as jnp
from jax import lax
from jax.experimental import pallas as pl
from jax.experimental.pallas import tpu as pltpu
from jax.sharding import PartitionSpec as P

HD = 128
WIN = 1024
BLK = 64
PAIR = 2 * HD
SCALE = 1.0 / math.sqrt(HD)
LOG2E = math.log2(math.e)


def diagonal(rows):
    zeros = jnp.zeros((BLK, HD), rows.dtype)
    top = jnp.concatenate([rows[:, :HD], zeros], axis=1)
    low = jnp.concatenate([zeros, rows[:, HD:]], axis=1)
    return jnp.concatenate([top, low], axis=0)


def attend_kernel(q_ref, g_ref, k_ref, v_ref, gq_ref, p_ref, ds_ref):
    keys = k_ref[...]
    last = (((1,), (1,)), ((), ()))
    scores = lax.dot_general(keys, diagonal(q_ref[...]), last, preferred_element_type=jnp.float32)
    dprobs = lax.dot_general(v_ref[...], diagonal(g_ref[...]), last, preferred_element_type=jnp.float32)
    top = jnp.max(scores, axis=0, keepdims=True)
    grown = jnp.exp2((scores - top) * (SCALE * LOG2E))
    probs = grown * (1.0 / jnp.sum(grown, axis=0, keepdims=True))
    probs_low = probs.astype(jnp.bfloat16)
    p_ref[...] = probs_low
    delta = jnp.sum(probs_low.astype(jnp.float32) * dprobs, axis=0, keepdims=True)
    dscores = (SCALE * probs * (dprobs - delta)).astype(jnp.bfloat16)
    ds_ref[...] = dscores
    both = lax.dot_general(dscores, keys, (((0,), (0,)), ((), ())), preferred_element_type=jnp.float32)
    gq_ref[:, :HD] = both[:BLK, :HD].astype(jnp.bfloat16)
    gq_ref[:, HD:] = both[BLK:, HD:].astype(jnp.bfloat16)


def attend(q_blk, g_blk, keys, values):
    width = q_blk.shape[1]
    steps = width // PAIR
    blk = pl.BlockSpec((BLK, PAIR), lambda i: (0, i))
    win = pl.BlockSpec((WIN, PAIR), lambda i: (0, i))
    prob = pl.BlockSpec((WIN, 2 * BLK), lambda i: (0, i))
    staged = jax.ShapeDtypeStruct((WIN, steps * 2 * BLK), jnp.bfloat16)
    return pl.pallas_call(
        attend_kernel,
        grid=(steps,),
        in_specs=[blk, blk, win, win],
        out_specs=[blk, prob, prob],
        out_shape=[jax.ShapeDtypeStruct((BLK, width), jnp.bfloat16), staged, staged],
        compiler_params=pltpu.CompilerParams(vmem_limit_bytes=32 << 20),
        cost_estimate=pl.CostEstimate(
            flops=8 * BLK * WIN * width, bytes_accessed=6 * WIN * width, transcendentals=BLK * WIN * width // HD
        ),
        name="attend",
    )(q_blk, g_blk, keys, values)


def event_kernel(p0_ref, ds0_ref, q0_ref, g0_ref, p1_ref, ds1_ref, q1_ref, g1_ref, gk_ref, gv_ref):
    def product(a0, a1, b0, b1):
        left = jnp.concatenate([a0[...], a1[...]], axis=1)
        right = jnp.concatenate([diagonal(b0[...]), diagonal(b1[...])], axis=0)
        return jnp.dot(left, right, preferred_element_type=jnp.float32).astype(jnp.bfloat16)

    gk_ref[...] = product(ds0_ref, ds1_ref, q0_ref, q1_ref)
    gv_ref[...] = product(p0_ref, p1_ref, g0_ref, g1_ref)


def event_grads(first, second):
    width = first[2].shape[1]
    steps = width // PAIR
    blk = pl.BlockSpec((BLK, PAIR), lambda i: (0, i))
    win = pl.BlockSpec((WIN, PAIR), lambda i: (0, i))
    prob = pl.BlockSpec((WIN, 2 * BLK), lambda i: (0, i))
    out = jax.ShapeDtypeStruct((WIN, width), jnp.bfloat16)
    return pl.pallas_call(
        event_kernel,
        grid=(steps,),
        in_specs=[prob, prob, blk, blk] * 2,
        out_specs=[win, win],
        out_shape=[out, out],
        compiler_params=pltpu.CompilerParams(vmem_limit_bytes=32 << 20),
        cost_estimate=pl.CostEstimate(
            flops=8 * BLK * WIN * width, bytes_accessed=8 * WIN * width, transcendentals=0
        ),
        name="event_grads",
    )(*first, *second)


def shards(queries, keys, values, out_grad, starts):
    del starts
    seq = lax.axis_size("seq")
    frames, width = queries.shape
    assert frames == 2 * BLK and keys.shape[0] == WIN and seq % 2 == 0
    inside = [(i, i ^ 1) for i in range(seq)]
    across = [(0, 0), (seq - 1, seq - 1)] + [(i, i + 1 if i % 2 else i - 1) for i in range(1, seq - 1)]
    even = lax.axis_index("seq") % 2 == 0
    core = lax.axis_index("tp")

    q_in = lax.dynamic_slice_in_dim(queries, jnp.where(even, BLK, 0), BLK, axis=0)
    q_out = lax.dynamic_slice_in_dim(queries, jnp.where(even, 0, BLK), BLK, axis=0)
    mine = lax.dynamic_slice_in_dim(out_grad, core * width, width, axis=1)
    other = lax.dynamic_slice_in_dim(out_grad, (1 - core) * width, width, axis=1)
    other = lax.ppermute(other, "tp", [(0, 1), (1, 0)])
    own_inside = even == (core == 1)
    g_in = jnp.where(own_inside, mine, other)
    g_out = jnp.where(own_inside, other, mine)

    q0 = lax.ppermute(q_in, "seq", inside)
    g0 = lax.ppermute(g_in, "seq", inside)
    q1 = lax.ppermute(q_out, "seq", across)
    g1 = lax.ppermute(g_out, "seq", across)
    gq0, p0, ds0 = attend(q0, g0, keys, values)
    back0 = lax.ppermute(gq0, "seq", inside)
    gq1, p1, ds1 = attend(q1, g1, keys, values)
    back1 = lax.ppermute(gq1, "seq", across)
    grad_keys, grad_values = event_grads((p0, ds0, q0, g0), (p1, ds1, q1, g1))
    grad_queries = jnp.concatenate([jnp.where(even, back1, back0), jnp.where(even, back0, back1)], axis=0)
    return grad_queries, grad_keys, grad_values


def solution(mesh):
    return jax.shard_map(
        shards,
        mesh=mesh,
        in_specs=(
            P(("group", "seq"), "tp"),
            P(("group", "seq"), "tp"),
            P(("group", "seq"), "tp"),
            P(("group", "seq", "tp"), None),
            P("group"),
        ),
        out_specs=(P(("group", "seq"), "tp"), P(("group", "seq"), "tp"), P(("group", "seq"), "tp")),
        check_vma=False,
    )
```

```python
import math

import jax
import jax.numpy as jnp
from jax import lax
from jax.experimental import pallas as pl
from jax.experimental.pallas import tpu as pltpu
from jax.sharding import PartitionSpec as P

HD = 128
WIN = 1024
BLK = 64
PAIR = 2 * HD
SCALE = 1.0 / math.sqrt(HD)
LOG2E = math.log2(math.e)
LAST = (((1,), (1,)), ((), ()))
FIRST = (((0,), (0,)), ((), ()))
WHOLE = pl.BlockSpec(memory_space=pltpu.VMEM)
RAW = pl.BlockSpec(memory_space=pltpu.HBM)


def params(mib):
    return pltpu.CompilerParams(vmem_limit_bytes=mib << 20)


def diagonal(rows):
    zeros = jnp.zeros((BLK, HD), rows.dtype)
    top = jnp.concatenate([rows[:, :HD], zeros], axis=1)
    low = jnp.concatenate([zeros, rows[:, HD:]], axis=1)
    return jnp.concatenate([top, low], axis=0)


def pack_kernel(q_ref, own_ref, other_ref, inside_ref, across_ref):
    width = q_ref.shape[1]
    odd = lax.axis_index("seq") % 2
    core = lax.axis_index("tp")
    cols = pl.ds(pl.multiple_of(core * width, HD), width)
    inside_ref[:BLK] = q_ref[pl.ds(pl.multiple_of((1 - odd) * BLK, BLK), BLK), :]
    across_ref[:BLK] = q_ref[pl.ds(pl.multiple_of(odd * BLK, BLK), BLK), :]

    @pl.when(core != odd)
    def _():
        inside_ref[BLK:] = own_ref[:, cols]
        across_ref[BLK:] = other_ref[:, cols]

    @pl.when(core == odd)
    def _():
        inside_ref[BLK:] = other_ref[:, cols]
        across_ref[BLK:] = own_ref[:, cols]


def pack(queries, own, other):
    part = jax.ShapeDtypeStruct(queries.shape, queries.dtype)
    return pl.pallas_call(
        pack_kernel,
        in_specs=[WHOLE] * 3,
        out_specs=[WHOLE] * 2,
        out_shape=[part] * 2,
        compiler_params=params(8),
        name="pack",
    )(queries, own, other)


def stage_kernel(k_hbm, v_hbm, k_ref, v_ref, sems):
    rows = WIN // 4
    moves = []
    for i in range(4):
        part = pl.ds(i * rows, rows)
        moves.append(pltpu.make_async_copy(k_hbm.at[part, :], k_ref.at[part, :], sems.at[0, i]))
        moves.append(pltpu.make_async_copy(v_hbm.at[part, :], v_ref.at[part, :], sems.at[1, i]))
    for move in moves:
        move.start()
    for move in moves:
        move.wait()


def stage(keys, values):
    part = jax.ShapeDtypeStruct(keys.shape, keys.dtype)
    return pl.pallas_call(
        stage_kernel,
        in_specs=[RAW] * 2,
        out_specs=[WHOLE] * 2,
        out_shape=[part] * 2,
        scratch_shapes=[pltpu.SemaphoreType.DMA((2, 4))],
        compiler_params=params(16),
        cost_estimate=pl.CostEstimate(flops=0, bytes_accessed=8 * keys.size, transcendentals=0),
        name="stage",
    )(keys, values)


def attend_kernel(m_ref, k_ref, v_ref, gq_ref, p_ref, ds_ref):
    pairs = m_ref.shape[1] // PAIR
    held = {}

    def products(j):
        cols = pl.ds(j * PAIR, PAIR)
        scores = lax.dot_general(
            k_ref[:, cols], diagonal(m_ref[:BLK, cols]), LAST, preferred_element_type=jnp.float32
        )
        dprobs = lax.dot_general(
            v_ref[:, cols], diagonal(m_ref[BLK:, cols]), LAST, preferred_element_type=jnp.float32
        )
        held[j] = (scores, jnp.max(scores, axis=0, keepdims=True), dprobs)

    def sums(j):
        scores, top, dprobs = held[j]
        grown = jnp.exp2((scores - top) * (SCALE * LOG2E))
        inverse = 1.0 / jnp.sum(grown, axis=0, keepdims=True)
        delta = jnp.sum(grown * dprobs, axis=0, keepdims=True) * inverse
        held[j] = (grown, inverse, dprobs, delta)

    def results(j):
        grown, inverse, dprobs, delta = held.pop(j)
        cols = pl.ds(j * 2 * BLK, 2 * BLK)
        p_ref[:, cols] = (grown * inverse).astype(jnp.bfloat16)
        dscores = (grown * (SCALE * inverse) * (dprobs - delta)).astype(jnp.bfloat16)
        ds_ref[:, cols] = dscores
        both = lax.dot_general(
            dscores, k_ref[:, pl.ds(j * PAIR, PAIR)], FIRST, preferred_element_type=jnp.float32
        )
        gq_ref[:, pl.ds(j * PAIR, HD)] = both[:BLK, :HD].astype(jnp.bfloat16)
        gq_ref[:, pl.ds(j * PAIR + HD, HD)] = both[BLK:, HD:].astype(jnp.bfloat16)

    for step in range(pairs + 2):
        for stage_of, lag in ((products, 0), (sums, 1), (results, 2)):
            if 0 <= step - lag < pairs:
                stage_of(step - lag)


def attend(message, keys, values):
    width = message.shape[1]
    staged = jax.ShapeDtypeStruct((WIN, width // HD * BLK), jnp.bfloat16)
    return pl.pallas_call(
        attend_kernel,
        in_specs=[WHOLE] * 3,
        out_specs=[WHOLE] * 3,
        out_shape=[jax.ShapeDtypeStruct((BLK, width), jnp.bfloat16), staged, staged],
        compiler_params=params(32),
        cost_estimate=pl.CostEstimate(
            flops=8 * BLK * WIN * width, bytes_accessed=6 * WIN * width, transcendentals=BLK * WIN * width // HD
        ),
        name="attend",
    )(message, keys, values)


def event_kernel(p0_ref, ds0_ref, m0_ref, p1_ref, ds1_ref, m1_ref, gk_ref, gv_ref):
    step = pl.program_id(0)
    probs = pl.ds(pl.multiple_of(step * 2 * BLK, 2 * BLK), 2 * BLK)
    cols = pl.ds(pl.multiple_of(step * PAIR, PAIR), PAIR)

    def product(a0, a1, b0, b1):
        left = jnp.concatenate([a0, a1], axis=1)
        right = jnp.concatenate([diagonal(b0), diagonal(b1)], axis=0)
        return jnp.dot(left, right, preferred_element_type=jnp.float32).astype(jnp.bfloat16)

    gk_ref[...] = product(ds0_ref[:, probs], ds1_ref[:, probs], m0_ref[:BLK, cols], m1_ref[:BLK, cols])
    gv_ref[...] = product(p0_ref[:, probs], p1_ref[:, probs], m0_ref[BLK:, cols], m1_ref[BLK:, cols])


def event_grads(*args):
    width = args[2].shape[1]
    win = pl.BlockSpec((WIN, PAIR), lambda i: (0, i))
    out = jax.ShapeDtypeStruct((WIN, width), jnp.bfloat16)
    return pl.pallas_call(
        event_kernel,
        grid=(width // PAIR,),
        in_specs=[WHOLE] * 6,
        out_specs=[win, win],
        out_shape=[out, out],
        compiler_params=params(32),
        cost_estimate=pl.CostEstimate(
            flops=8 * BLK * WIN * width, bytes_accessed=8 * WIN * width, transcendentals=0
        ),
        name="event_grads",
    )(*args)


def join_kernel(inside_ref, across_ref, out_hbm, sems):
    odd = lax.axis_index("seq") % 2
    moves = [
        pltpu.make_async_copy(
            ref, out_hbm.at[pl.ds(pl.multiple_of(row * BLK, BLK), BLK), :], sems.at[i]
        )
        for i, (ref, row) in enumerate(((inside_ref, 1 - odd), (across_ref, odd)))
    ]
    for move in moves:
        move.start()
    for move in moves:
        move.wait()


def join(back_inside, back_across):
    width = back_inside.shape[1]
    return pl.pallas_call(
        join_kernel,
        in_specs=[WHOLE] * 2,
        out_specs=RAW,
        out_shape=jax.ShapeDtypeStruct((2 * BLK, width), back_inside.dtype),
        scratch_shapes=[pltpu.SemaphoreType.DMA((2,))],
        compiler_params=params(8),
        name="join",
    )(back_inside, back_across)


def shards(queries, keys, values, out_grad, starts):
    del starts
    seq = lax.axis_size("seq")
    frames, width = queries.shape
    assert frames == 2 * BLK and keys.shape[0] == WIN and seq % 2 == 0
    inside = [(i, i ^ 1) for i in range(seq)]
    across = [(0, 0), (seq - 1, seq - 1)] + [(i, i + 1 if i % 2 else i - 1) for i in range(1, seq - 1)]

    other = lax.ppermute(out_grad, "tp", [(0, 1), (1, 0)])
    first, second = pack(queries, out_grad, other)
    first = lax.ppermute(first, "seq", inside)
    second = lax.ppermute(second, "seq", across)
    keys, values = stage(keys, values)
    gq0, p0, ds0 = attend(first, keys, values)
    back0 = lax.ppermute(gq0, "seq", inside)
    gq1, p1, ds1 = attend(second, keys, values)
    back1 = lax.ppermute(gq1, "seq", across)
    grad_keys, grad_values = event_grads(p0, ds0, first, p1, ds1, second)
    return join(back0, back1), grad_keys, grad_values


def solution(mesh):
    return jax.shard_map(
        shards,
        mesh=mesh,
        in_specs=(
            P(("group", "seq"), "tp"),
            P(("group", "seq"), "tp"),
            P(("group", "seq"), "tp"),
            P(("group", "seq", "tp"), None),
            P("group"),
        ),
        out_specs=(P(("group", "seq"), "tp"), P(("group", "seq"), "tp"), P(("group", "seq"), "tp")),
        check_vma=False,
    )
```

```python
import math

import jax
import jax.numpy as jnp
from jax import lax
from jax.experimental import pallas as pl
from jax.experimental.pallas import tpu as pltpu
from jax.sharding import PartitionSpec as P

HD = 128
WIN = 1024
BLK = 64
PAIR = 2 * HD
SCALE = 1.0 / math.sqrt(HD)
LOG2E = math.log2(math.e)
LAST = (((1,), (1,)), ((), ()))
FIRST = (((0,), (0,)), ((), ()))
WHOLE = pl.BlockSpec(memory_space=pltpu.VMEM)
RAW = pl.BlockSpec(memory_space=pltpu.HBM)


def params(mib):
    return pltpu.CompilerParams(vmem_limit_bytes=mib << 20)


def diagonal(rows):
    zeros = jnp.zeros((BLK, HD), rows.dtype)
    top = jnp.concatenate([rows[:, :HD], zeros], axis=1)
    low = jnp.concatenate([zeros, rows[:, HD:]], axis=1)
    return jnp.concatenate([top, low], axis=0)


def load_kernel(q_hbm, g_hbm, q_ref, g_ref, sems):
    moves = [
        pltpu.make_async_copy(q_hbm, q_ref, sems.at[0]),
        pltpu.make_async_copy(g_hbm, g_ref, sems.at[1]),
    ]
    for move in moves:
        move.start()
    for move in moves:
        move.wait()


def load(queries, out_grad):
    return pl.pallas_call(
        load_kernel,
        in_specs=[RAW] * 2,
        out_specs=[WHOLE] * 2,
        out_shape=[jax.ShapeDtypeStruct(x.shape, x.dtype) for x in (queries, out_grad)],
        scratch_shapes=[pltpu.SemaphoreType.DMA((2,))],
        compiler_params=params(8),
        name="load",
    )(queries, out_grad)


def pack_kernel(q_ref, own_ref, other_ref, inside_ref, across_ref):
    width = q_ref.shape[1]
    odd = lax.axis_index("seq") % 2
    core = lax.axis_index("tp")
    cols = pl.ds(pl.multiple_of(core * width, HD), width)
    inside_ref[:BLK] = q_ref[pl.ds(pl.multiple_of((1 - odd) * BLK, BLK), BLK), :]
    across_ref[:BLK] = q_ref[pl.ds(pl.multiple_of(odd * BLK, BLK), BLK), :]

    @pl.when(core != odd)
    def _():
        inside_ref[BLK:] = own_ref[:, cols]
        across_ref[BLK:] = other_ref[:, cols]

    @pl.when(core == odd)
    def _():
        inside_ref[BLK:] = other_ref[:, cols]
        across_ref[BLK:] = own_ref[:, cols]


def pack(queries, own, other):
    part = jax.ShapeDtypeStruct(queries.shape, queries.dtype)
    return pl.pallas_call(
        pack_kernel,
        in_specs=[WHOLE] * 3,
        out_specs=[WHOLE] * 2,
        out_shape=[part] * 2,
        compiler_params=params(8),
        name="pack",
    )(queries, own, other)


def stage_kernel(k_hbm, v_hbm, k_ref, v_ref, sems):
    rows = WIN // 4
    moves = []
    for i in range(4):
        part = pl.ds(i * rows, rows)
        moves.append(pltpu.make_async_copy(k_hbm.at[part, :], k_ref.at[part, :], sems.at[0, i]))
        moves.append(pltpu.make_async_copy(v_hbm.at[part, :], v_ref.at[part, :], sems.at[1, i]))
    for move in moves:
        move.start()
    for move in moves:
        move.wait()


def stage(keys, values):
    part = jax.ShapeDtypeStruct(keys.shape, keys.dtype)
    return pl.pallas_call(
        stage_kernel,
        in_specs=[RAW] * 2,
        out_specs=[WHOLE] * 2,
        out_shape=[part] * 2,
        scratch_shapes=[pltpu.SemaphoreType.DMA((2, 4))],
        compiler_params=params(16),
        cost_estimate=pl.CostEstimate(flops=0, bytes_accessed=8 * keys.size, transcendentals=0),
        name="stage",
    )(keys, values)


def attend_kernel(m_ref, k_ref, v_ref, gq_ref, p_ref, ds_ref):
    pairs = m_ref.shape[1] // PAIR
    held = {}

    def products(j):
        cols = pl.ds(j * PAIR, PAIR)
        scores = lax.dot_general(
            k_ref[:, cols], diagonal(m_ref[:BLK, cols]), LAST, preferred_element_type=jnp.float32
        )
        dprobs = lax.dot_general(
            v_ref[:, cols], diagonal(m_ref[BLK:, cols]), LAST, preferred_element_type=jnp.float32
        )
        held[j] = (scores, jnp.max(scores, axis=0, keepdims=True), dprobs)

    def sums(j):
        scores, top, dprobs = held[j]
        grown = jnp.exp2((scores - top) * (SCALE * LOG2E))
        inverse = 1.0 / jnp.sum(grown, axis=0, keepdims=True)
        delta = jnp.sum(grown * dprobs, axis=0, keepdims=True) * inverse
        held[j] = (grown, inverse, dprobs, delta)

    def results(j):
        grown, inverse, dprobs, delta = held.pop(j)
        cols = pl.ds(j * 2 * BLK, 2 * BLK)
        p_ref[:, cols] = (grown * inverse).astype(jnp.bfloat16)
        dscores = (grown * (SCALE * inverse) * (dprobs - delta)).astype(jnp.bfloat16)
        ds_ref[:, cols] = dscores
        both = lax.dot_general(
            dscores, k_ref[:, pl.ds(j * PAIR, PAIR)], FIRST, preferred_element_type=jnp.float32
        )
        gq_ref[:, pl.ds(j * PAIR, HD)] = both[:BLK, :HD].astype(jnp.bfloat16)
        gq_ref[:, pl.ds(j * PAIR + HD, HD)] = both[BLK:, HD:].astype(jnp.bfloat16)

    for step in range(pairs + 2):
        for stage_of, lag in ((products, 0), (sums, 1), (results, 2)):
            if 0 <= step - lag < pairs:
                stage_of(step - lag)


def attend(message, keys, values):
    width = message.shape[1]
    staged = jax.ShapeDtypeStruct((WIN, width // HD * BLK), jnp.bfloat16)
    return pl.pallas_call(
        attend_kernel,
        in_specs=[WHOLE] * 3,
        out_specs=[WHOLE] * 3,
        out_shape=[jax.ShapeDtypeStruct((BLK, width), jnp.bfloat16), staged, staged],
        compiler_params=params(32),
        cost_estimate=pl.CostEstimate(
            flops=8 * BLK * WIN * width, bytes_accessed=6 * WIN * width, transcendentals=BLK * WIN * width // HD
        ),
        name="attend",
    )(message, keys, values)


def event_kernel(p0_ref, ds0_ref, m0_ref, p1_ref, ds1_ref, m1_ref, gk_ref, gv_ref):
    step = pl.program_id(0)
    probs = pl.ds(pl.multiple_of(step * 2 * BLK, 2 * BLK), 2 * BLK)
    cols = pl.ds(pl.multiple_of(step * PAIR, PAIR), PAIR)

    def product(a0, a1, b0, b1):
        left = jnp.concatenate([a0, a1], axis=1)
        right = jnp.concatenate([diagonal(b0), diagonal(b1)], axis=0)
        return jnp.dot(left, right, preferred_element_type=jnp.float32).astype(jnp.bfloat16)

    gk_ref[...] = product(ds0_ref[:, probs], ds1_ref[:, probs], m0_ref[:BLK, cols], m1_ref[:BLK, cols])
    gv_ref[...] = product(p0_ref[:, probs], p1_ref[:, probs], m0_ref[BLK:, cols], m1_ref[BLK:, cols])


def event_grads(*args):
    width = args[2].shape[1]
    win = pl.BlockSpec((WIN, PAIR), lambda i: (0, i))
    out = jax.ShapeDtypeStruct((WIN, width), jnp.bfloat16)
    return pl.pallas_call(
        event_kernel,
        grid=(width // PAIR,),
        in_specs=[WHOLE] * 6,
        out_specs=[win, win],
        out_shape=[out, out],
        compiler_params=params(32),
        cost_estimate=pl.CostEstimate(
            flops=8 * BLK * WIN * width, bytes_accessed=8 * WIN * width, transcendentals=0
        ),
        name="event_grads",
    )(*args)


def join_kernel(inside_ref, across_ref, out_hbm, sems):
    odd = lax.axis_index("seq") % 2
    moves = [
        pltpu.make_async_copy(
            ref, out_hbm.at[pl.ds(pl.multiple_of(row * BLK, BLK), BLK), :], sems.at[i]
        )
        for i, (ref, row) in enumerate(((inside_ref, 1 - odd), (across_ref, odd)))
    ]
    for move in moves:
        move.start()
    for move in moves:
        move.wait()


def join(back_inside, back_across):
    width = back_inside.shape[1]
    return pl.pallas_call(
        join_kernel,
        in_specs=[WHOLE] * 2,
        out_specs=RAW,
        out_shape=jax.ShapeDtypeStruct((2 * BLK, width), back_inside.dtype),
        scratch_shapes=[pltpu.SemaphoreType.DMA((2,))],
        compiler_params=params(8),
        name="join",
    )(back_inside, back_across)


def shards(queries, keys, values, out_grad, starts):
    del starts
    seq = lax.axis_size("seq")
    frames, width = queries.shape
    assert frames == 2 * BLK and keys.shape[0] == WIN and seq % 2 == 0
    inside = [(i, i ^ 1) for i in range(seq)]
    across = [(0, 0), (seq - 1, seq - 1)] + [(i, i + 1 if i % 2 else i - 1) for i in range(1, seq - 1)]

    other = lax.ppermute(out_grad, "tp", [(0, 1), (1, 0)])
    first, second = pack(*load(queries, out_grad), other)
    first = lax.ppermute(first, "seq", inside)
    second = lax.ppermute(second, "seq", across)
    keys, values = stage(keys, values)
    gq0, p0, ds0 = attend(first, keys, values)
    back0 = lax.ppermute(gq0, "seq", inside)
    gq1, p1, ds1 = attend(second, keys, values)
    back1 = lax.ppermute(gq1, "seq", across)
    grad_keys, grad_values = event_grads(p0, ds0, first, p1, ds1, second)
    return join(back0, back1), grad_keys, grad_values


def solution(mesh):
    return jax.shard_map(
        shards,
        mesh=mesh,
        in_specs=(
            P(("group", "seq"), "tp"),
            P(("group", "seq"), "tp"),
            P(("group", "seq"), "tp"),
            P(("group", "seq", "tp"), None),
            P("group"),
        ),
        out_specs=(P(("group", "seq"), "tp"), P(("group", "seq"), "tp"), P(("group", "seq"), "tp")),
        check_vma=False,
    )
```

```python
import math

import jax
import jax.numpy as jnp
from jax import lax
from jax.experimental import pallas as pl
from jax.experimental.pallas import tpu as pltpu
from jax.sharding import PartitionSpec as P

HD = 128
WIN = 1024
BLK = 64
PAIR = 2 * HD
SCALE = 1.0 / math.sqrt(HD)
LOG2E = math.log2(math.e)
LAST = (((1,), (1,)), ((), ()))
FIRST = (((0,), (0,)), ((), ()))
WHOLE = pl.BlockSpec(memory_space=pltpu.VMEM)
RAW = pl.BlockSpec(memory_space=pltpu.HBM)


def params(mib):
    return pltpu.CompilerParams(vmem_limit_bytes=mib << 20)


def diagonal(rows):
    zeros = jnp.zeros((BLK, HD), rows.dtype)
    top = jnp.concatenate([rows[:, :HD], zeros], axis=1)
    low = jnp.concatenate([zeros, rows[:, HD:]], axis=1)
    return jnp.concatenate([top, low], axis=0)


def load_kernel(q_hbm, g_hbm, q_ref, g_ref, sems):
    moves = [
        pltpu.make_async_copy(q_hbm, q_ref, sems.at[0]),
        pltpu.make_async_copy(g_hbm, g_ref, sems.at[1]),
    ]
    for move in moves:
        move.start()
    for move in moves:
        move.wait()


def load(queries, out_grad):
    return pl.pallas_call(
        load_kernel,
        in_specs=[RAW] * 2,
        out_specs=[WHOLE] * 2,
        out_shape=[jax.ShapeDtypeStruct(x.shape, x.dtype) for x in (queries, out_grad)],
        scratch_shapes=[pltpu.SemaphoreType.DMA((2,))],
        compiler_params=params(8),
        name="load",
    )(queries, out_grad)


def pack_kernel(q_ref, own_ref, other_ref, inside_ref, across_ref):
    width = q_ref.shape[1]
    odd = lax.axis_index("seq") % 2
    core = lax.axis_index("tp")
    cols = pl.ds(pl.multiple_of(core * width, HD), width)
    inside_ref[:BLK] = q_ref[pl.ds(pl.multiple_of((1 - odd) * BLK, BLK), BLK), :]
    across_ref[:BLK] = q_ref[pl.ds(pl.multiple_of(odd * BLK, BLK), BLK), :]

    @pl.when(core != odd)
    def _():
        inside_ref[BLK:] = own_ref[:, cols]
        across_ref[BLK:] = other_ref[:, cols]

    @pl.when(core == odd)
    def _():
        inside_ref[BLK:] = other_ref[:, cols]
        across_ref[BLK:] = own_ref[:, cols]


def pack(queries, own, other):
    part = jax.ShapeDtypeStruct(queries.shape, queries.dtype)
    return pl.pallas_call(
        pack_kernel,
        in_specs=[WHOLE] * 3,
        out_specs=[WHOLE] * 2,
        out_shape=[part] * 2,
        compiler_params=params(8),
        name="pack",
    )(queries, own, other)


def stage_kernel(k_hbm, v_hbm, k_ref, v_ref, sems):
    rows = WIN // 4
    moves = []
    for i in range(4):
        part = pl.ds(i * rows, rows)
        moves.append(pltpu.make_async_copy(k_hbm.at[part, :], k_ref.at[part, :], sems.at[0, i]))
        moves.append(pltpu.make_async_copy(v_hbm.at[part, :], v_ref.at[part, :], sems.at[1, i]))
    for move in moves:
        move.start()
    for move in moves:
        move.wait()


def stage(keys, values):
    part = jax.ShapeDtypeStruct(keys.shape, keys.dtype)
    return pl.pallas_call(
        stage_kernel,
        in_specs=[RAW] * 2,
        out_specs=[WHOLE] * 2,
        out_shape=[part] * 2,
        scratch_shapes=[pltpu.SemaphoreType.DMA((2, 4))],
        compiler_params=params(16),
        cost_estimate=pl.CostEstimate(flops=0, bytes_accessed=8 * keys.size, transcendentals=0),
        name="stage",
    )(keys, values)


def at_end():
    index = lax.axis_index("seq")
    return (index == 0) | (index == lax.axis_size("seq") - 1)


def attend_inside_kernel(m_ref, k_ref, v_ref, gq_ref, p_ref, ds_ref):
    attend_body(m_ref, k_ref, v_ref, gq_ref, p_ref, ds_ref)


def attend_across_kernel(own_ref, received_ref, k_ref, v_ref, gq_ref, p_ref, ds_ref, m_ref):
    @pl.when(at_end())
    def _():
        m_ref[...] = own_ref[...]

    @pl.when(jnp.logical_not(at_end()))
    def _():
        m_ref[...] = received_ref[...]

    attend_body(m_ref, k_ref, v_ref, gq_ref, p_ref, ds_ref)


def attend_body(m_ref, k_ref, v_ref, gq_ref, p_ref, ds_ref):
    pairs = m_ref.shape[1] // PAIR
    held = {}

    def products(j):
        cols = pl.ds(j * PAIR, PAIR)
        scores = lax.dot_general(
            k_ref[:, cols], diagonal(m_ref[:BLK, cols]), LAST, preferred_element_type=jnp.float32
        )
        dprobs = lax.dot_general(
            v_ref[:, cols], diagonal(m_ref[BLK:, cols]), LAST, preferred_element_type=jnp.float32
        )
        held[j] = (scores, jnp.max(scores, axis=0, keepdims=True), dprobs)

    def sums(j):
        scores, top, dprobs = held[j]
        grown = jnp.exp2((scores - top) * (SCALE * LOG2E))
        inverse = 1.0 / jnp.sum(grown, axis=0, keepdims=True)
        delta = jnp.sum(grown * dprobs, axis=0, keepdims=True) * inverse
        held[j] = (grown, inverse, dprobs, delta)

    def results(j):
        grown, inverse, dprobs, delta = held.pop(j)
        cols = pl.ds(j * 2 * BLK, 2 * BLK)
        p_ref[:, cols] = (grown * inverse).astype(jnp.bfloat16)
        dscores = (grown * (SCALE * inverse) * (dprobs - delta)).astype(jnp.bfloat16)
        ds_ref[:, cols] = dscores
        both = lax.dot_general(
            dscores, k_ref[:, pl.ds(j * PAIR, PAIR)], FIRST, preferred_element_type=jnp.float32
        )
        gq_ref[:, pl.ds(j * PAIR, HD)] = both[:BLK, :HD].astype(jnp.bfloat16)
        gq_ref[:, pl.ds(j * PAIR + HD, HD)] = both[BLK:, HD:].astype(jnp.bfloat16)

    for step in range(pairs + 2):
        for stage_of, lag in ((products, 0), (sums, 1), (results, 2)):
            if 0 <= step - lag < pairs:
                stage_of(step - lag)


def attend(kernel, messages, keys, values):
    width = keys.shape[1]
    staged = jax.ShapeDtypeStruct((WIN, width // HD * BLK), jnp.bfloat16)
    shapes = [jax.ShapeDtypeStruct((BLK, width), jnp.bfloat16), staged, staged]
    if len(messages) == 2:
        shapes.append(jax.ShapeDtypeStruct(messages[0].shape, messages[0].dtype))
    return pl.pallas_call(
        kernel,
        in_specs=[WHOLE] * (len(messages) + 2),
        out_specs=[WHOLE] * len(shapes),
        out_shape=shapes,
        compiler_params=params(32),
        cost_estimate=pl.CostEstimate(
            flops=8 * BLK * WIN * width, bytes_accessed=6 * WIN * width, transcendentals=BLK * WIN * width // HD
        ),
        name="attend",
    )(*messages, keys, values)


def event_kernel(p0_ref, ds0_ref, m0_ref, p1_ref, ds1_ref, m1_ref, gk_ref, gv_ref):
    step = pl.program_id(0)
    probs = pl.ds(pl.multiple_of(step * 2 * BLK, 2 * BLK), 2 * BLK)
    cols = pl.ds(pl.multiple_of(step * PAIR, PAIR), PAIR)

    def product(a0, a1, b0, b1):
        left = jnp.concatenate([a0, a1], axis=1)
        right = jnp.concatenate([diagonal(b0), diagonal(b1)], axis=0)
        return jnp.dot(left, right, preferred_element_type=jnp.float32).astype(jnp.bfloat16)

    gk_ref[...] = product(ds0_ref[:, probs], ds1_ref[:, probs], m0_ref[:BLK, cols], m1_ref[:BLK, cols])
    gv_ref[...] = product(p0_ref[:, probs], p1_ref[:, probs], m0_ref[BLK:, cols], m1_ref[BLK:, cols])


def event_grads(*args):
    width = args[2].shape[1]
    win = pl.BlockSpec((WIN, PAIR), lambda i: (0, i))
    out = jax.ShapeDtypeStruct((WIN, width), jnp.bfloat16)
    return pl.pallas_call(
        event_kernel,
        grid=(width // PAIR,),
        in_specs=[WHOLE] * 6,
        out_specs=[win, win],
        out_shape=[out, out],
        compiler_params=params(32),
        cost_estimate=pl.CostEstimate(
            flops=8 * BLK * WIN * width, bytes_accessed=8 * WIN * width, transcendentals=0
        ),
        name="event_grads",
    )(*args)


def join_across_kernel(across_ref, own_ref, out_hbm, sem):
    odd = lax.axis_index("seq") % 2
    rows = out_hbm.at[pl.ds(pl.multiple_of(odd * BLK, BLK), BLK), :]

    @pl.when(at_end())
    def _():
        pltpu.make_async_copy(own_ref, rows, sem).start()

    @pl.when(jnp.logical_not(at_end()))
    def _():
        pltpu.make_async_copy(across_ref, rows, sem).start()

    pltpu.make_async_copy(across_ref, rows, sem).wait()


def join_inside_kernel(inside_ref, half_hbm, out_hbm, sem):
    odd = lax.axis_index("seq") % 2
    move = pltpu.make_async_copy(
        inside_ref, out_hbm.at[pl.ds(pl.multiple_of((1 - odd) * BLK, BLK), BLK), :], sem
    )
    move.start()
    move.wait()


def join_across(back_across, own_across):
    width = back_across.shape[1]
    return pl.pallas_call(
        join_across_kernel,
        in_specs=[WHOLE] * 2,
        out_specs=RAW,
        out_shape=jax.ShapeDtypeStruct((2 * BLK, width), back_across.dtype),
        scratch_shapes=[pltpu.SemaphoreType.DMA],
        compiler_params=params(8),
        name="join_across",
    )(back_across, own_across)


def join_inside(back_inside, half):
    return pl.pallas_call(
        join_inside_kernel,
        in_specs=[WHOLE, RAW],
        out_specs=RAW,
        out_shape=jax.ShapeDtypeStruct(half.shape, half.dtype),
        scratch_shapes=[pltpu.SemaphoreType.DMA],
        input_output_aliases={1: 0},
        compiler_params=params(8),
        name="join_inside",
    )(back_inside, half)


def shards(queries, keys, values, out_grad, starts):
    del starts
    seq = lax.axis_size("seq")
    frames, width = queries.shape
    assert frames == 2 * BLK and keys.shape[0] == WIN and seq % 2 == 0 and lax.axis_size("tp") == 2
    inside = [(i, i ^ 1) for i in range(seq)]
    across = [(0, 1), (1, 0), (2 * seq - 2, 2 * seq - 1), (2 * seq - 1, 2 * seq - 2)]
    for i in range(1, seq - 1):
        partner = i + 1 if i % 2 else i - 1
        across += [(2 * i + core, 2 * partner + core) for core in range(2)]

    other = lax.ppermute(out_grad, "tp", [(0, 1), (1, 0)])
    first, second = pack(*load(queries, out_grad), other)
    got_first = lax.ppermute(first, "seq", inside)
    got_second = lax.ppermute(second, ("seq", "tp"), across)
    keys, values = stage(keys, values)
    gq1, p1, ds1, used = attend(attend_across_kernel, [second, got_second], keys, values)
    back1 = lax.ppermute(gq1, ("seq", "tp"), across)
    gq0, p0, ds0 = attend(attend_inside_kernel, [got_first], keys, values)
    back0 = lax.ppermute(gq0, "seq", inside)
    grad_keys, grad_values = event_grads(p0, ds0, got_first, p1, ds1, used)
    return join_inside(back0, join_across(back1, gq1)), grad_keys, grad_values


def solution(mesh):
    return jax.shard_map(
        shards,
        mesh=mesh,
        in_specs=(
            P(("group", "seq"), "tp"),
            P(("group", "seq"), "tp"),
            P(("group", "seq"), "tp"),
            P(("group", "seq", "tp"), None),
            P("group"),
        ),
        out_specs=(P(("group", "seq"), "tp"), P(("group", "seq"), "tp"), P(("group", "seq"), "tp")),
        check_vma=False,
    )
```

```python
import math

import jax
import jax.numpy as jnp
from jax import lax
from jax.experimental import pallas as pl
from jax.experimental.pallas import tpu as pltpu
from jax.sharding import PartitionSpec as P

HD = 128
WIN = 1024
BLK = 64
PAIR = 2 * HD
SCALE = 1.0 / math.sqrt(HD)
LOG2E = math.log2(math.e)
LAST = (((1,), (1,)), ((), ()))
FIRST = (((0,), (0,)), ((), ()))
WHOLE = pl.BlockSpec(memory_space=pltpu.VMEM)
RAW = pl.BlockSpec(memory_space=pltpu.HBM)


def params(mib):
    return pltpu.CompilerParams(vmem_limit_bytes=mib << 20)


def diagonal(rows):
    zeros = jnp.zeros((BLK, HD), rows.dtype)
    top = jnp.concatenate([rows[:, :HD], zeros], axis=1)
    low = jnp.concatenate([zeros, rows[:, HD:]], axis=1)
    return jnp.concatenate([top, low], axis=0)


def load_kernel(q_hbm, g_hbm, q_ref, g_ref, sems):
    moves = [
        pltpu.make_async_copy(q_hbm, q_ref, sems.at[0]),
        pltpu.make_async_copy(g_hbm, g_ref, sems.at[1]),
    ]
    for move in moves:
        move.start()
    for move in moves:
        move.wait()


def load(queries, out_grad):
    return pl.pallas_call(
        load_kernel,
        in_specs=[RAW] * 2,
        out_specs=[WHOLE] * 2,
        out_shape=[jax.ShapeDtypeStruct(x.shape, x.dtype) for x in (queries, out_grad)],
        scratch_shapes=[pltpu.SemaphoreType.DMA((2,))],
        compiler_params=params(8),
        name="load",
    )(queries, out_grad)


def pack_kernel(q_ref, own_ref, other_ref, left_ref, right_ref, across_ref):
    width = q_ref.shape[1]
    odd = lax.axis_index("seq") % 2
    core = lax.axis_index("tp")
    cols = pl.ds(pl.multiple_of(core * width, HD), width)
    half = width // 2
    rows = pl.ds(pl.multiple_of((1 - odd) * BLK, BLK), BLK)
    left_ref[:BLK] = q_ref[rows, :half]
    right_ref[:BLK] = q_ref[rows, half:]
    across_ref[:BLK] = q_ref[pl.ds(pl.multiple_of(odd * BLK, BLK), BLK), :]
    lefts = pl.ds(pl.multiple_of(core * width, HD), half)
    rights = pl.ds(pl.multiple_of(core * width + half, HD), half)

    @pl.when(core != odd)
    def _():
        left_ref[BLK:] = own_ref[:, lefts]
        right_ref[BLK:] = own_ref[:, rights]
        across_ref[BLK:] = other_ref[:, cols]

    @pl.when(core == odd)
    def _():
        left_ref[BLK:] = other_ref[:, lefts]
        right_ref[BLK:] = other_ref[:, rights]
        across_ref[BLK:] = own_ref[:, cols]


def pack(queries, own, other):
    rows, width = queries.shape
    return pl.pallas_call(
        pack_kernel,
        in_specs=[WHOLE] * 3,
        out_specs=[WHOLE] * 3,
        out_shape=[jax.ShapeDtypeStruct((rows, cols), queries.dtype) for cols in (width // 2, width // 2, width)],
        compiler_params=params(8),
        name="pack",
    )(queries, own, other)


def stage_kernel(k_hbm, v_hbm, k_ref, v_ref, sems):
    rows = WIN // 4
    moves = []
    for i in range(4):
        part = pl.ds(i * rows, rows)
        moves.append(pltpu.make_async_copy(k_hbm.at[part, :], k_ref.at[part, :], sems.at[0, i]))
        moves.append(pltpu.make_async_copy(v_hbm.at[part, :], v_ref.at[part, :], sems.at[1, i]))
    for move in moves:
        move.start()
    for move in moves:
        move.wait()


def stage(keys, values):
    part = jax.ShapeDtypeStruct(keys.shape, keys.dtype)
    return pl.pallas_call(
        stage_kernel,
        in_specs=[RAW] * 2,
        out_specs=[WHOLE] * 2,
        out_shape=[part] * 2,
        scratch_shapes=[pltpu.SemaphoreType.DMA((2, 4))],
        compiler_params=params(16),
        cost_estimate=pl.CostEstimate(flops=0, bytes_accessed=8 * keys.size, transcendentals=0),
        name="stage",
    )(keys, values)


def at_end():
    index = lax.axis_index("seq")
    return (index == 0) | (index == lax.axis_size("seq") - 1)


def attend_left_kernel(m_ref, after_ref, k_ref, v_ref, gq_ref, p_ref, ds_ref):
    del after_ref
    attend_body(m_ref, k_ref, v_ref, gq_ref, p_ref, ds_ref, 0)


def attend_right_kernel(m_ref, left_ref, k_ref, v_ref, gq_ref, p_ref, ds_ref):
    start = left_ref.shape[1]
    gq_ref[:, :start] = left_ref[...]
    attend_body(m_ref, k_ref, v_ref, gq_ref.at[:, start:], p_ref, ds_ref, start)


def attend_across_kernel(own_ref, received_ref, k_ref, v_ref, gq_ref, p_ref, ds_ref, m_ref):
    @pl.when(at_end())
    def _():
        m_ref[...] = own_ref[...]

    @pl.when(jnp.logical_not(at_end()))
    def _():
        m_ref[...] = received_ref[...]

    attend_body(m_ref, k_ref, v_ref, gq_ref, p_ref, ds_ref, 0)


def attend_body(m_ref, k_ref, v_ref, gq_ref, p_ref, ds_ref, start):
    pairs = m_ref.shape[1] // PAIR
    held = {}

    def products(j):
        cols = pl.ds(j * PAIR, PAIR)
        window = pl.ds(start + j * PAIR, PAIR)
        scores = lax.dot_general(
            k_ref[:, window], diagonal(m_ref[:BLK, cols]), LAST, preferred_element_type=jnp.float32
        )
        dprobs = lax.dot_general(
            v_ref[:, window], diagonal(m_ref[BLK:, cols]), LAST, preferred_element_type=jnp.float32
        )
        held[j] = (scores, jnp.max(scores, axis=0, keepdims=True), dprobs)

    def sums(j):
        scores, top, dprobs = held[j]
        grown = jnp.exp2((scores - top) * (SCALE * LOG2E))
        inverse = 1.0 / jnp.sum(grown, axis=0, keepdims=True)
        delta = jnp.sum(grown * dprobs, axis=0, keepdims=True) * inverse
        held[j] = (grown, inverse, dprobs, delta)

    def results(j):
        grown, inverse, dprobs, delta = held.pop(j)
        cols = pl.ds(j * 2 * BLK, 2 * BLK)
        p_ref[:, cols] = (grown * inverse).astype(jnp.bfloat16)
        dscores = (grown * (SCALE * inverse) * (dprobs - delta)).astype(jnp.bfloat16)
        ds_ref[:, cols] = dscores
        both = lax.dot_general(
            dscores, k_ref[:, pl.ds(start + j * PAIR, PAIR)], FIRST, preferred_element_type=jnp.float32
        )
        gq_ref[:, pl.ds(j * PAIR, HD)] = both[:BLK, :HD].astype(jnp.bfloat16)
        gq_ref[:, pl.ds(j * PAIR + HD, HD)] = both[BLK:, HD:].astype(jnp.bfloat16)

    for step in range(pairs + 2):
        for stage_of, lag in ((products, 0), (sums, 1), (results, 2)):
            if 0 <= step - lag < pairs:
                stage_of(step - lag)


def attend(kernel, message, others, keys, values, width, copied=False):
    heads = message.shape[1] // HD
    staged = jax.ShapeDtypeStruct((WIN, heads * BLK), jnp.bfloat16)
    shapes = [jax.ShapeDtypeStruct((BLK, width), jnp.bfloat16), staged, staged]
    if copied:
        shapes.append(jax.ShapeDtypeStruct(message.shape, message.dtype))
    return pl.pallas_call(
        kernel,
        in_specs=[WHOLE] * (len(others) + 3),
        out_specs=[WHOLE] * len(shapes),
        out_shape=shapes,
        compiler_params=params(32),
        cost_estimate=pl.CostEstimate(
            flops=8 * BLK * WIN * HD * heads, bytes_accessed=6 * WIN * HD * heads, transcendentals=BLK * WIN * heads
        ),
        name="attend",
    )(message, *others, keys, values)


def event_kernel(pl_ref, dsl_ref, ml_ref, pr_ref, dsr_ref, mr_ref, p1_ref, ds1_ref, m1_ref, gk_hbm, gv_hbm, gk_ref, gv_ref, sems):
    parts = sems.shape[1]
    rows = WIN // parts
    moves = []
    pairs = gk_ref.shape[1] // PAIR
    half = pairs // 2
    for out, (left_ref, right_ref, a1, held, hbm, low) in enumerate(
        ((dsl_ref, dsr_ref, ds1_ref, gk_ref, gk_hbm, 0), (pl_ref, pr_ref, p1_ref, gv_ref, gv_hbm, BLK))
    ):
        block = pl.ds(low, BLK)
        rights = []
        for j in range(pairs):
            inside = (ml_ref if j < half else mr_ref)[block, pl.ds(j % half * PAIR, PAIR)]
            across = m1_ref[block, pl.ds(j * PAIR, PAIR)]
            rights.append(jnp.concatenate([diagonal(inside), diagonal(across)], axis=0))
        for part in range(parts):
            here = pl.ds(part * rows, rows)
            for j, right in enumerate(rights):
                inside = (left_ref if j < half else right_ref)[here, pl.ds(j % half * 2 * BLK, 2 * BLK)]
                left = jnp.concatenate([inside, a1[here, pl.ds(j * 2 * BLK, 2 * BLK)]], axis=1)
                held[here, pl.ds(j * PAIR, PAIR)] = jnp.dot(
                    left, right, preferred_element_type=jnp.float32
                ).astype(jnp.bfloat16)
            move = pltpu.make_async_copy(held.at[here, :], hbm.at[here, :], sems.at[out, part])
            move.start()
            moves.append(move)
    for move in moves:
        move.wait()


def event_grads(*args):
    width = args[-1].shape[1]
    out = jax.ShapeDtypeStruct((WIN, width), jnp.bfloat16)
    return pl.pallas_call(
        event_kernel,
        in_specs=[WHOLE] * 9,
        out_specs=[RAW] * 2,
        out_shape=[out] * 2,
        scratch_shapes=[pltpu.VMEM((WIN, width), jnp.bfloat16)] * 2 + [pltpu.SemaphoreType.DMA((2, 4))],
        compiler_params=params(32),
        cost_estimate=pl.CostEstimate(
            flops=8 * BLK * WIN * width, bytes_accessed=8 * WIN * width, transcendentals=0
        ),
        name="event_grads",
    )(*args)


def join_across_kernel(across_ref, own_ref, out_hbm, sem):
    odd = lax.axis_index("seq") % 2
    rows = out_hbm.at[pl.ds(pl.multiple_of(odd * BLK, BLK), BLK), :]

    @pl.when(at_end())
    def _():
        pltpu.make_async_copy(own_ref, rows, sem).start()

    @pl.when(jnp.logical_not(at_end()))
    def _():
        pltpu.make_async_copy(across_ref, rows, sem).start()

    pltpu.make_async_copy(across_ref, rows, sem).wait()


def join_inside_kernel(inside_ref, half_hbm, out_hbm, sem):
    odd = lax.axis_index("seq") % 2
    move = pltpu.make_async_copy(
        inside_ref, out_hbm.at[pl.ds(pl.multiple_of((1 - odd) * BLK, BLK), BLK), :], sem
    )
    move.start()
    move.wait()


def join_across(back_across, own_across):
    width = back_across.shape[1]
    return pl.pallas_call(
        join_across_kernel,
        in_specs=[WHOLE] * 2,
        out_specs=RAW,
        out_shape=jax.ShapeDtypeStruct((2 * BLK, width), back_across.dtype),
        scratch_shapes=[pltpu.SemaphoreType.DMA],
        compiler_params=params(8),
        name="join_across",
    )(back_across, own_across)


def join_inside(back_inside, half):
    return pl.pallas_call(
        join_inside_kernel,
        in_specs=[WHOLE, RAW],
        out_specs=RAW,
        out_shape=jax.ShapeDtypeStruct(half.shape, half.dtype),
        scratch_shapes=[pltpu.SemaphoreType.DMA],
        input_output_aliases={1: 0},
        compiler_params=params(8),
        name="join_inside",
    )(back_inside, half)


def shards(queries, keys, values, out_grad, starts):
    del starts
    seq = lax.axis_size("seq")
    frames, width = queries.shape
    assert frames == 2 * BLK and keys.shape[0] == WIN and seq % 2 == 0 and lax.axis_size("tp") == 2
    inside = [(i, i ^ 1) for i in range(seq)]
    across = [(0, 1), (1, 0), (2 * seq - 2, 2 * seq - 1), (2 * seq - 1, 2 * seq - 2)]
    for i in range(1, seq - 1):
        partner = i + 1 if i % 2 else i - 1
        across += [(2 * i + core, 2 * partner + core) for core in range(2)]

    other = lax.ppermute(out_grad, "tp", [(0, 1), (1, 0)])
    left, right, second = pack(*load(queries, out_grad), other)
    got_second = lax.ppermute(second, ("seq", "tp"), across)
    got_left = lax.ppermute(left, "seq", inside)
    got_right = lax.ppermute(right, "seq", inside)
    keys, values = stage(keys, values)
    gq1, p1, ds1, used = attend(attend_across_kernel, second, [got_second], keys, values, width, True)
    back1 = lax.ppermute(gq1, ("seq", "tp"), across)
    gql, *lefts = attend(attend_left_kernel, got_left, [p1], keys, values, width // 2)
    gq0, *rights = attend(attend_right_kernel, got_right, [gql], keys, values, width)
    back0 = lax.ppermute(gq0, "seq", inside)
    grad_keys, grad_values = event_grads(*lefts, got_left, *rights, got_right, p1, ds1, used)
    return join_inside(back0, join_across(back1, gq1)), grad_keys, grad_values


def solution(mesh):
    return jax.shard_map(
        shards,
        mesh=mesh,
        in_specs=(
            P(("group", "seq"), "tp"),
            P(("group", "seq"), "tp"),
            P(("group", "seq"), "tp"),
            P(("group", "seq", "tp"), None),
            P("group"),
        ),
        out_specs=(P(("group", "seq"), "tp"), P(("group", "seq"), "tp"), P(("group", "seq"), "tp")),
        check_vma=False,
    )
```

```python
import math

import jax
import jax.numpy as jnp
from jax import lax
from jax.experimental import pallas as pl
from jax.experimental.pallas import tpu as pltpu
from jax.sharding import PartitionSpec as P

HD = 128
WIN = 1024
BLK = 64
PAIR = 2 * HD
SCALE = 1.0 / math.sqrt(HD)
LOG2E = math.log2(math.e)
LAST = (((1,), (1,)), ((), ()))
FIRST = (((0,), (0,)), ((), ()))
WHOLE = pl.BlockSpec(memory_space=pltpu.VMEM)
RAW = pl.BlockSpec(memory_space=pltpu.HBM)


def params(mib):
    return pltpu.CompilerParams(vmem_limit_bytes=mib << 20)


def pinned(array):
    return pltpu.with_memory_space_constraint(array, pltpu.HBM)


def diagonal(rows):
    zeros = jnp.zeros((BLK, HD), rows.dtype)
    top = jnp.concatenate([rows[:, :HD], zeros], axis=1)
    low = jnp.concatenate([zeros, rows[:, HD:]], axis=1)
    return jnp.concatenate([top, low], axis=0)


def load_kernel(q_hbm, g_hbm, q_ref, g_ref, sems):
    moves = [
        pltpu.make_async_copy(q_hbm, q_ref, sems.at[0]),
        pltpu.make_async_copy(g_hbm, g_ref, sems.at[1]),
    ]
    for move in moves:
        move.start()
    for move in moves:
        move.wait()


def load(queries, out_grad):
    return pl.pallas_call(
        load_kernel,
        in_specs=[RAW] * 2,
        out_specs=[WHOLE] * 2,
        out_shape=[jax.ShapeDtypeStruct(x.shape, x.dtype) for x in (queries, out_grad)],
        scratch_shapes=[pltpu.SemaphoreType.DMA((2,))],
        compiler_params=params(8),
        name="load",
    )(pinned(queries), pinned(out_grad))


def pack_kernel(q_ref, own_ref, other_ref, left_ref, right_ref, across_ref):
    width = q_ref.shape[1]
    odd = lax.axis_index("seq") % 2
    core = lax.axis_index("tp")
    cols = pl.ds(pl.multiple_of(core * width, HD), width)
    half = width // 2
    rows = pl.ds(pl.multiple_of((1 - odd) * BLK, BLK), BLK)
    left_ref[:BLK] = q_ref[rows, :half]
    right_ref[:BLK] = q_ref[rows, half:]
    across_ref[:BLK] = q_ref[pl.ds(pl.multiple_of(odd * BLK, BLK), BLK), :]
    lefts = pl.ds(pl.multiple_of(core * width, HD), half)
    rights = pl.ds(pl.multiple_of(core * width + half, HD), half)

    @pl.when(core != odd)
    def _():
        left_ref[BLK:] = own_ref[:, lefts]
        right_ref[BLK:] = own_ref[:, rights]
        across_ref[BLK:] = other_ref[:, cols]

    @pl.when(core == odd)
    def _():
        left_ref[BLK:] = other_ref[:, lefts]
        right_ref[BLK:] = other_ref[:, rights]
        across_ref[BLK:] = own_ref[:, cols]


def pack(queries, own, other):
    rows, width = queries.shape
    return pl.pallas_call(
        pack_kernel,
        in_specs=[WHOLE] * 3,
        out_specs=[WHOLE] * 3,
        out_shape=[jax.ShapeDtypeStruct((rows, cols), queries.dtype) for cols in (width // 2, width // 2, width)],
        compiler_params=params(8),
        name="pack",
    )(queries, own, other)


def stage_kernel(k_hbm, v_hbm, k_ref, v_ref, sems):
    rows = WIN // 4
    moves = []
    for i in range(4):
        part = pl.ds(i * rows, rows)
        moves.append(pltpu.make_async_copy(k_hbm.at[part, :], k_ref.at[part, :], sems.at[0, i]))
        moves.append(pltpu.make_async_copy(v_hbm.at[part, :], v_ref.at[part, :], sems.at[1, i]))
    for move in moves:
        move.start()
    for move in moves:
        move.wait()


def stage(keys, values):
    part = jax.ShapeDtypeStruct(keys.shape, keys.dtype)
    return pl.pallas_call(
        stage_kernel,
        in_specs=[RAW] * 2,
        out_specs=[WHOLE] * 2,
        out_shape=[part] * 2,
        scratch_shapes=[pltpu.SemaphoreType.DMA((2, 4))],
        compiler_params=params(16),
        cost_estimate=pl.CostEstimate(flops=0, bytes_accessed=8 * keys.size, transcendentals=0),
        name="stage",
    )(pinned(keys), pinned(values))


def at_end():
    index = lax.axis_index("seq")
    return (index == 0) | (index == lax.axis_size("seq") - 1)


def attend_left_kernel(m_ref, after_ref, k_ref, v_ref, gq_ref, p_ref, ds_ref):
    del after_ref
    attend_body(m_ref, k_ref, v_ref, gq_ref, p_ref, ds_ref, 0)


def attend_right_kernel(m_ref, left_ref, k_ref, v_ref, gq_ref, p_ref, ds_ref):
    start = left_ref.shape[1]
    gq_ref[:, :start] = left_ref[...]
    attend_body(m_ref, k_ref, v_ref, gq_ref.at[:, start:], p_ref, ds_ref, start)


def attend_across_kernel(own_ref, received_ref, k_ref, v_ref, gq_ref, p_ref, ds_ref, m_ref):
    @pl.when(at_end())
    def _():
        m_ref[...] = own_ref[...]

    @pl.when(jnp.logical_not(at_end()))
    def _():
        m_ref[...] = received_ref[...]

    attend_body(m_ref, k_ref, v_ref, gq_ref, p_ref, ds_ref, 0)


def attend_body(m_ref, k_ref, v_ref, gq_ref, p_ref, ds_ref, start):
    pairs = m_ref.shape[1] // PAIR
    held = {}

    def products(j):
        cols = pl.ds(j * PAIR, PAIR)
        window = pl.ds(start + j * PAIR, PAIR)
        scores = lax.dot_general(
            k_ref[:, window], diagonal(m_ref[:BLK, cols]), LAST, preferred_element_type=jnp.float32
        )
        dprobs = lax.dot_general(
            v_ref[:, window], diagonal(m_ref[BLK:, cols]), LAST, preferred_element_type=jnp.float32
        )
        held[j] = (scores, jnp.max(scores, axis=0, keepdims=True), dprobs)

    def sums(j):
        scores, top, dprobs = held[j]
        grown = jnp.exp2((scores - top) * (SCALE * LOG2E))
        inverse = 1.0 / jnp.sum(grown, axis=0, keepdims=True)
        delta = jnp.sum(grown * dprobs, axis=0, keepdims=True) * inverse
        held[j] = (grown, inverse, dprobs, delta)

    def results(j):
        grown, inverse, dprobs, delta = held.pop(j)
        cols = pl.ds(j * 2 * BLK, 2 * BLK)
        p_ref[:, cols] = (grown * inverse).astype(jnp.bfloat16)
        dscores = (grown * (SCALE * inverse) * (dprobs - delta)).astype(jnp.bfloat16)
        ds_ref[:, cols] = dscores
        both = lax.dot_general(
            dscores, k_ref[:, pl.ds(start + j * PAIR, PAIR)], FIRST, preferred_element_type=jnp.float32
        )
        gq_ref[:, pl.ds(j * PAIR, HD)] = both[:BLK, :HD].astype(jnp.bfloat16)
        gq_ref[:, pl.ds(j * PAIR + HD, HD)] = both[BLK:, HD:].astype(jnp.bfloat16)

    for step in range(pairs + 2):
        for stage_of, lag in ((products, 0), (sums, 1), (results, 2)):
            if 0 <= step - lag < pairs:
                stage_of(step - lag)


def after_kernel(array_ref, message_ref, out_ref):
    del message_ref
    out_ref[...] = array_ref[...]


def after(array, message):
    return pl.pallas_call(
        after_kernel,
        in_specs=[WHOLE] * 2,
        out_specs=WHOLE,
        out_shape=jax.ShapeDtypeStruct(array.shape, array.dtype),
        compiler_params=params(8),
        name="after",
    )(array, message)


def attend(kernel, message, others, keys, values, width, copied=None):
    heads = message.shape[1] // HD
    staged = jax.ShapeDtypeStruct((WIN, heads * BLK), jnp.bfloat16)
    shapes = [jax.ShapeDtypeStruct((BLK, width), jnp.bfloat16), staged, staged]
    if copied is not None:
        shapes.append(jax.ShapeDtypeStruct(copied.shape, copied.dtype))
    return pl.pallas_call(
        kernel,
        in_specs=[WHOLE] * (len(others) + 3),
        out_specs=[WHOLE] * len(shapes),
        out_shape=shapes,
        compiler_params=params(32),
        cost_estimate=pl.CostEstimate(
            flops=8 * BLK * WIN * HD * heads, bytes_accessed=6 * WIN * HD * heads, transcendentals=BLK * WIN * heads
        ),
        name="attend",
    )(message, *others, keys, values)


def event_kernel(pl_ref, dsl_ref, ml_ref, pr_ref, dsr_ref, mr_ref, p1_ref, ds1_ref, m1_ref, gk_hbm, gv_hbm, gk_ref, gv_ref, sems):
    parts = sems.shape[1]
    rows = WIN // parts
    moves = []
    pairs = gk_ref.shape[1] // PAIR
    half = pairs // 2
    for out, (left_ref, right_ref, a1, held, hbm, low) in enumerate(
        ((dsl_ref, dsr_ref, ds1_ref, gk_ref, gk_hbm, 0), (pl_ref, pr_ref, p1_ref, gv_ref, gv_hbm, BLK))
    ):
        block = pl.ds(low, BLK)
        rights = []
        for j in range(pairs):
            inside = (ml_ref if j < half else mr_ref)[block, pl.ds(j % half * PAIR, PAIR)]
            across = m1_ref[block, pl.ds(j * PAIR, PAIR)]
            rights.append(jnp.concatenate([diagonal(inside), diagonal(across)], axis=0))
        for part in range(parts):
            here = pl.ds(part * rows, rows)
            for j, right in enumerate(rights):
                inside = (left_ref if j < half else right_ref)[here, pl.ds(j % half * 2 * BLK, 2 * BLK)]
                left = jnp.concatenate([inside, a1[here, pl.ds(j * 2 * BLK, 2 * BLK)]], axis=1)
                held[here, pl.ds(j * PAIR, PAIR)] = jnp.dot(
                    left, right, preferred_element_type=jnp.float32
                ).astype(jnp.bfloat16)
            move = pltpu.make_async_copy(held.at[here, :], hbm.at[here, :], sems.at[out, part])
            move.start()
            moves.append(move)
    for move in moves:
        move.wait()


def event_grads(*args):
    width = args[-1].shape[1]
    out = jax.ShapeDtypeStruct((WIN, width), jnp.bfloat16)
    return pl.pallas_call(
        event_kernel,
        in_specs=[WHOLE] * 9,
        out_specs=[RAW] * 2,
        out_shape=[out] * 2,
        scratch_shapes=[pltpu.VMEM((WIN, width), jnp.bfloat16)] * 2 + [pltpu.SemaphoreType.DMA((2, 4))],
        compiler_params=params(32),
        cost_estimate=pl.CostEstimate(
            flops=8 * BLK * WIN * width, bytes_accessed=8 * WIN * width, transcendentals=0
        ),
        name="event_grads",
    )(*args)


def join_across_kernel(across_ref, own_ref, out_hbm, sem):
    odd = lax.axis_index("seq") % 2
    rows = out_hbm.at[pl.ds(pl.multiple_of(odd * BLK, BLK), BLK), :]

    @pl.when(at_end())
    def _():
        pltpu.make_async_copy(own_ref, rows, sem).start()

    @pl.when(jnp.logical_not(at_end()))
    def _():
        pltpu.make_async_copy(across_ref, rows, sem).start()

    pltpu.make_async_copy(across_ref, rows, sem).wait()


def join_inside_kernel(inside_ref, half_hbm, out_hbm, sem):
    odd = lax.axis_index("seq") % 2
    move = pltpu.make_async_copy(
        inside_ref, out_hbm.at[pl.ds(pl.multiple_of((1 - odd) * BLK, BLK), BLK), :], sem
    )
    move.start()
    move.wait()


def join_across(back_across, own_across):
    width = back_across.shape[1]
    return pl.pallas_call(
        join_across_kernel,
        in_specs=[WHOLE] * 2,
        out_specs=RAW,
        out_shape=jax.ShapeDtypeStruct((2 * BLK, width), back_across.dtype),
        scratch_shapes=[pltpu.SemaphoreType.DMA],
        compiler_params=params(8),
        name="join_across",
    )(back_across, own_across)


def join_inside(back_inside, half):
    return pl.pallas_call(
        join_inside_kernel,
        in_specs=[WHOLE, RAW],
        out_specs=RAW,
        out_shape=jax.ShapeDtypeStruct(half.shape, half.dtype),
        scratch_shapes=[pltpu.SemaphoreType.DMA],
        input_output_aliases={1: 0},
        compiler_params=params(8),
        name="join_inside",
    )(back_inside, half)


def shards(queries, keys, values, out_grad, starts):
    del starts
    seq = lax.axis_size("seq")
    frames, width = queries.shape
    assert frames == 2 * BLK and keys.shape[0] == WIN and seq % 2 == 0 and lax.axis_size("tp") == 2
    inside = [(i, i ^ 1) for i in range(seq)]
    across = [(0, 1), (1, 0), (2 * seq - 2, 2 * seq - 1), (2 * seq - 1, 2 * seq - 2)]
    for i in range(1, seq - 1):
        partner = i + 1 if i % 2 else i - 1
        across += [(2 * i + core, 2 * partner + core) for core in range(2)]

    other = lax.ppermute(out_grad, "tp", [(0, 1), (1, 0)])
    left, right, second = pack(*load(queries, out_grad), other)
    got_second = lax.ppermute(second, ("seq", "tp"), across)
    got_left = lax.ppermute(left, "seq", inside)
    got_right = lax.ppermute(right, "seq", inside)
    keys, values = stage(keys, values)
    gq1, p1, ds1, used = attend(attend_across_kernel, second, [got_second], keys, values, width, second)
    sent = after(gq1, got_left)
    back1 = lax.ppermute(sent, ("seq", "tp"), across)
    gql, *lefts = attend(attend_left_kernel, got_left, [sent], keys, values, width // 2)
    gq0, *rights = attend(attend_right_kernel, got_right, [gql], keys, values, width)
    back0 = lax.ppermute(gq0, "seq", inside)
    grad_keys, grad_values = event_grads(*lefts, got_left, *rights, got_right, p1, ds1, used)
    return join_inside(back0, join_across(back1, gq1)), grad_keys, grad_values


def solution(mesh):
    return jax.shard_map(
        shards,
        mesh=mesh,
        in_specs=(
            P(("group", "seq"), "tp"),
            P(("group", "seq"), "tp"),
            P(("group", "seq"), "tp"),
            P(("group", "seq", "tp"), None),
            P("group"),
        ),
        out_specs=(P(("group", "seq"), "tp"), P(("group", "seq"), "tp"), P(("group", "seq"), "tp")),
        check_vma=False,
    )
```

```python
import math

import jax
import jax.numpy as jnp
from jax import lax
from jax.experimental import pallas as pl
from jax.experimental.pallas import tpu as pltpu
from jax.sharding import PartitionSpec as P

HD = 128
WIN = 1024
BLK = 64
PAIR = 2 * HD
SCALE = 1.0 / math.sqrt(HD)
LOG2E = math.log2(math.e)
LAST = (((1,), (1,)), ((), ()))
FIRST = (((0,), (0,)), ((), ()))
WHOLE = pl.BlockSpec(memory_space=pltpu.VMEM)
RAW = pl.BlockSpec(memory_space=pltpu.HBM)


def params(mib):
    return pltpu.CompilerParams(vmem_limit_bytes=mib << 20)


def pinned(array):
    return pltpu.with_memory_space_constraint(array, pltpu.HBM)


def diagonal(rows):
    zeros = jnp.zeros((BLK, HD), rows.dtype)
    top = jnp.concatenate([rows[:, :HD], zeros], axis=1)
    low = jnp.concatenate([zeros, rows[:, HD:]], axis=1)
    return jnp.concatenate([top, low], axis=0)


def load_kernel(q_hbm, g_hbm, q_ref, g_ref, sems):
    moves = [
        pltpu.make_async_copy(q_hbm, q_ref, sems.at[0]),
        pltpu.make_async_copy(g_hbm, g_ref, sems.at[1]),
    ]
    for move in moves:
        move.start()
    for move in moves:
        move.wait()


def load(queries, out_grad):
    return pl.pallas_call(
        load_kernel,
        in_specs=[RAW] * 2,
        out_specs=[WHOLE] * 2,
        out_shape=[jax.ShapeDtypeStruct(x.shape, x.dtype) for x in (queries, out_grad)],
        scratch_shapes=[pltpu.SemaphoreType.DMA((2,))],
        compiler_params=params(8),
        name="load",
    )(pinned(queries), pinned(out_grad))


def pack_kernel(q_ref, own_ref, other_ref, left_ref, right_ref, across_ref):
    width = q_ref.shape[1]
    odd = lax.axis_index("seq") % 2
    core = lax.axis_index("tp")
    cols = pl.ds(pl.multiple_of(core * width, HD), width)
    half = width // 2
    rows = pl.ds(pl.multiple_of((1 - odd) * BLK, BLK), BLK)
    left_ref[:BLK] = q_ref[rows, :half]
    right_ref[:BLK] = q_ref[rows, half:]
    across_ref[:BLK] = q_ref[pl.ds(pl.multiple_of(odd * BLK, BLK), BLK), :]
    lefts = pl.ds(pl.multiple_of(core * width, HD), half)
    rights = pl.ds(pl.multiple_of(core * width + half, HD), half)

    @pl.when(core != odd)
    def _():
        left_ref[BLK:] = own_ref[:, lefts]
        right_ref[BLK:] = own_ref[:, rights]
        across_ref[BLK:] = other_ref[:, cols]

    @pl.when(core == odd)
    def _():
        left_ref[BLK:] = other_ref[:, lefts]
        right_ref[BLK:] = other_ref[:, rights]
        across_ref[BLK:] = own_ref[:, cols]


def pack(queries, own, other):
    rows, width = queries.shape
    return pl.pallas_call(
        pack_kernel,
        in_specs=[WHOLE] * 3,
        out_specs=[WHOLE] * 3,
        out_shape=[jax.ShapeDtypeStruct((rows, cols), queries.dtype) for cols in (width // 2, width // 2, width)],
        compiler_params=params(8),
        name="pack",
    )(queries, own, other)


def stage_kernel(k_hbm, v_hbm, k_ref, v_ref, sems):
    rows = WIN // 4
    moves = []
    for i in range(4):
        part = pl.ds(i * rows, rows)
        moves.append(pltpu.make_async_copy(k_hbm.at[part, :], k_ref.at[part, :], sems.at[0, i]))
        moves.append(pltpu.make_async_copy(v_hbm.at[part, :], v_ref.at[part, :], sems.at[1, i]))
    for move in moves:
        move.start()
    for move in moves:
        move.wait()


def stage(keys, values):
    part = jax.ShapeDtypeStruct(keys.shape, keys.dtype)
    return pl.pallas_call(
        stage_kernel,
        in_specs=[RAW] * 2,
        out_specs=[WHOLE] * 2,
        out_shape=[part] * 2,
        scratch_shapes=[pltpu.SemaphoreType.DMA((2, 4))],
        compiler_params=params(16),
        cost_estimate=pl.CostEstimate(flops=0, bytes_accessed=8 * keys.size, transcendentals=0),
        name="stage",
    )(pinned(keys), pinned(values))


def at_end():
    index = lax.axis_index("seq")
    return (index == 0) | (index == lax.axis_size("seq") - 1)


def attend_left_kernel(m_ref, after_ref, k_ref, v_ref, gq_ref, p_ref, ds_ref):
    del after_ref
    attend_body(m_ref, k_ref, v_ref, gq_ref, p_ref, ds_ref, 0)


def attend_right_kernel(m_ref, left_ref, k_ref, v_ref, gq_ref, p_ref, ds_ref):
    start = left_ref.shape[1]
    gq_ref[:, :start] = left_ref[...]
    attend_body(m_ref, k_ref, v_ref, gq_ref.at[:, start:], p_ref, ds_ref, start)


def attend_across_kernel(own_ref, received_ref, k_ref, v_ref, gq_ref, p_ref, ds_ref, m_ref):
    @pl.when(at_end())
    def _():
        m_ref[...] = own_ref[...]

    @pl.when(jnp.logical_not(at_end()))
    def _():
        m_ref[...] = received_ref[...]

    attend_body(m_ref, k_ref, v_ref, gq_ref, p_ref, ds_ref, 0)


def attend_body(m_ref, k_ref, v_ref, gq_ref, p_ref, ds_ref, start):
    pairs = m_ref.shape[1] // PAIR
    held = {}

    def products(j):
        cols = pl.ds(j * PAIR, PAIR)
        window = pl.ds(start + j * PAIR, PAIR)
        scores = lax.dot_general(
            k_ref[:, window], diagonal(m_ref[:BLK, cols]), LAST, preferred_element_type=jnp.float32
        )
        dprobs = lax.dot_general(
            v_ref[:, window], diagonal(m_ref[BLK:, cols]), LAST, preferred_element_type=jnp.float32
        )
        held[j] = (scores, jnp.max(scores, axis=0, keepdims=True), dprobs)

    def sums(j):
        scores, top, dprobs = held[j]
        grown = jnp.exp2((scores - top) * (SCALE * LOG2E))
        inverse = 1.0 / jnp.sum(grown, axis=0, keepdims=True)
        delta = jnp.sum(grown * dprobs, axis=0, keepdims=True) * inverse
        held[j] = (grown, inverse, dprobs, delta)

    def results(j):
        grown, inverse, dprobs, delta = held.pop(j)
        cols = pl.ds(j * 2 * BLK, 2 * BLK)
        probs = grown * inverse
        p_ref[:, cols] = probs.astype(jnp.bfloat16)
        dscores = (probs * ((dprobs - delta) * SCALE)).astype(jnp.bfloat16)
        ds_ref[:, cols] = dscores
        both = lax.dot_general(
            dscores, k_ref[:, pl.ds(start + j * PAIR, PAIR)], FIRST, preferred_element_type=jnp.float32
        )
        gq_ref[:, pl.ds(j * PAIR, HD)] = both[:BLK, :HD].astype(jnp.bfloat16)
        gq_ref[:, pl.ds(j * PAIR + HD, HD)] = both[BLK:, HD:].astype(jnp.bfloat16)

    for step in range(pairs + 2):
        for stage_of, lag in ((products, 0), (sums, 1), (results, 2)):
            if 0 <= step - lag < pairs:
                stage_of(step - lag)


def after_kernel(array_ref, message_ref, out_ref):
    del message_ref
    out_ref[...] = array_ref[...]


def after(array, message):
    return pl.pallas_call(
        after_kernel,
        in_specs=[WHOLE] * 2,
        out_specs=WHOLE,
        out_shape=jax.ShapeDtypeStruct(array.shape, array.dtype),
        compiler_params=params(8),
        name="after",
    )(array, message)


def attend(kernel, message, others, keys, values, width, copied=None):
    heads = message.shape[1] // HD
    staged = jax.ShapeDtypeStruct((WIN, heads * BLK), jnp.bfloat16)
    shapes = [jax.ShapeDtypeStruct((BLK, width), jnp.bfloat16), staged, staged]
    if copied is not None:
        shapes.append(jax.ShapeDtypeStruct(copied.shape, copied.dtype))
    return pl.pallas_call(
        kernel,
        in_specs=[WHOLE] * (len(others) + 3),
        out_specs=[WHOLE] * len(shapes),
        out_shape=shapes,
        compiler_params=params(32),
        cost_estimate=pl.CostEstimate(
            flops=8 * BLK * WIN * HD * heads, bytes_accessed=6 * WIN * HD * heads, transcendentals=BLK * WIN * heads
        ),
        name="attend",
    )(message, *others, keys, values)


def event_kernel(pl_ref, dsl_ref, ml_ref, pr_ref, dsr_ref, mr_ref, p1_ref, ds1_ref, m1_ref, back_ref, own_ref, gk_hbm, gv_hbm, gq_hbm, gk_ref, gv_ref, sems, sem):
    odd = lax.axis_index("seq") % 2
    block_rows = gq_hbm.at[pl.ds(pl.multiple_of(odd * BLK, BLK), BLK), :]

    @pl.when(at_end())
    def _():
        pltpu.make_async_copy(own_ref, block_rows, sem).start()

    @pl.when(jnp.logical_not(at_end()))
    def _():
        pltpu.make_async_copy(back_ref, block_rows, sem).start()

    parts = sems.shape[1]
    rows = WIN // parts
    moves = []
    pairs = gk_ref.shape[1] // PAIR
    half = pairs // 2
    for out, (left_ref, right_ref, a1, held, hbm, low) in enumerate(
        ((dsl_ref, dsr_ref, ds1_ref, gk_ref, gk_hbm, 0), (pl_ref, pr_ref, p1_ref, gv_ref, gv_hbm, BLK))
    ):
        block = pl.ds(low, BLK)
        rights = []
        for j in range(pairs):
            inside = (ml_ref if j < half else mr_ref)[block, pl.ds(j % half * PAIR, PAIR)]
            across = m1_ref[block, pl.ds(j * PAIR, PAIR)]
            rights.append(jnp.concatenate([diagonal(inside), diagonal(across)], axis=0))
        for part in range(parts):
            here = pl.ds(part * rows, rows)
            for j, right in enumerate(rights):
                inside = (left_ref if j < half else right_ref)[here, pl.ds(j % half * 2 * BLK, 2 * BLK)]
                left = jnp.concatenate([inside, a1[here, pl.ds(j * 2 * BLK, 2 * BLK)]], axis=1)
                held[here, pl.ds(j * PAIR, PAIR)] = jnp.dot(
                    left, right, preferred_element_type=jnp.float32
                ).astype(jnp.bfloat16)
            move = pltpu.make_async_copy(held.at[here, :], hbm.at[here, :], sems.at[out, part])
            move.start()
            moves.append(move)
    for move in moves:
        move.wait()
    pltpu.make_async_copy(back_ref, block_rows, sem).wait()


def event_grads(*args):
    width = args[-1].shape[1]
    out = jax.ShapeDtypeStruct((WIN, width), jnp.bfloat16)
    return pl.pallas_call(
        event_kernel,
        in_specs=[WHOLE] * 11,
        out_specs=[RAW] * 3,
        out_shape=[out, out, jax.ShapeDtypeStruct((2 * BLK, width), jnp.bfloat16)],
        scratch_shapes=[pltpu.VMEM((WIN, width), jnp.bfloat16)] * 2 + [pltpu.SemaphoreType.DMA((2, 4)), pltpu.SemaphoreType.DMA],
        compiler_params=params(32),
        cost_estimate=pl.CostEstimate(
            flops=8 * BLK * WIN * width, bytes_accessed=8 * WIN * width, transcendentals=0
        ),
        name="event_grads",
    )(*args)


def join_inside_kernel(inside_ref, half_hbm, out_hbm, sem):
    odd = lax.axis_index("seq") % 2
    move = pltpu.make_async_copy(
        inside_ref, out_hbm.at[pl.ds(pl.multiple_of((1 - odd) * BLK, BLK), BLK), :], sem
    )
    move.start()
    move.wait()


def join_inside(back_inside, half):
    return pl.pallas_call(
        join_inside_kernel,
        in_specs=[WHOLE, RAW],
        out_specs=RAW,
        out_shape=jax.ShapeDtypeStruct(half.shape, half.dtype),
        scratch_shapes=[pltpu.SemaphoreType.DMA],
        input_output_aliases={1: 0},
        compiler_params=params(8),
        name="join_inside",
    )(back_inside, half)


def shards(queries, keys, values, out_grad, starts):
    del starts
    seq = lax.axis_size("seq")
    frames, width = queries.shape
    assert frames == 2 * BLK and keys.shape[0] == WIN and seq % 2 == 0 and lax.axis_size("tp") == 2
    inside = [(i, i ^ 1) for i in range(seq)]
    across = [(0, 1), (1, 0), (2 * seq - 2, 2 * seq - 1), (2 * seq - 1, 2 * seq - 2)]
    for i in range(1, seq - 1):
        partner = i + 1 if i % 2 else i - 1
        across += [(2 * i + core, 2 * partner + core) for core in range(2)]

    other = lax.ppermute(out_grad, "tp", [(0, 1), (1, 0)])
    left, right, second = pack(*load(queries, out_grad), other)
    got_second = lax.ppermute(second, ("seq", "tp"), across)
    got_left = lax.ppermute(left, "seq", inside)
    got_right = lax.ppermute(right, "seq", inside)
    keys, values = stage(keys, values)
    gq1, p1, ds1, used = attend(attend_across_kernel, second, [got_second], keys, values, width, second)
    sent = after(gq1, got_left)
    back1 = lax.ppermute(sent, ("seq", "tp"), across)
    gql, *lefts = attend(attend_left_kernel, got_left, [sent], keys, values, width // 2)
    gq0, *rights = attend(attend_right_kernel, got_right, [gql], keys, values, width)
    back0 = lax.ppermute(gq0, "seq", inside)
    grad_keys, grad_values, half = event_grads(*lefts, got_left, *rights, got_right, p1, ds1, used, back1, gq1)
    return join_inside(back0, half), grad_keys, grad_values


def solution(mesh):
    return jax.shard_map(
        shards,
        mesh=mesh,
        in_specs=(
            P(("group", "seq"), "tp"),
            P(("group", "seq"), "tp"),
            P(("group", "seq"), "tp"),
            P(("group", "seq", "tp"), None),
            P("group"),
        ),
        out_specs=(P(("group", "seq"), "tp"), P(("group", "seq"), "tp"), P(("group", "seq"), "tp")),
        check_vma=False,
    )
```

```python
import math

import jax
import jax.numpy as jnp
from jax import lax
from jax.experimental import pallas as pl
from jax.experimental.pallas import tpu as pltpu
from jax.sharding import PartitionSpec as P

HD = 128
WIN = 1024
BLK = 64
PAIR = 2 * HD
SCALE = 1.0 / math.sqrt(HD)
LOG2E = math.log2(math.e)
LAST = (((1,), (1,)), ((), ()))
FIRST = (((0,), (0,)), ((), ()))
WHOLE = pl.BlockSpec(memory_space=pltpu.VMEM)
RAW = pl.BlockSpec(memory_space=pltpu.HBM)


def params(mib):
    return pltpu.CompilerParams(vmem_limit_bytes=mib << 20)


def pinned(array):
    return pltpu.with_memory_space_constraint(array, pltpu.HBM)


def diagonal(rows):
    zeros = jnp.zeros((BLK, HD), rows.dtype)
    top = jnp.concatenate([rows[:, :HD], zeros], axis=1)
    low = jnp.concatenate([zeros, rows[:, HD:]], axis=1)
    return jnp.concatenate([top, low], axis=0)


def load_kernel(q_hbm, g_hbm, q_ref, g_ref, sems):
    moves = [
        pltpu.make_async_copy(q_hbm, q_ref, sems.at[0]),
        pltpu.make_async_copy(g_hbm, g_ref, sems.at[1]),
    ]
    for move in moves:
        move.start()
    for move in moves:
        move.wait()


def load(queries, out_grad):
    return pl.pallas_call(
        load_kernel,
        in_specs=[RAW] * 2,
        out_specs=[WHOLE] * 2,
        out_shape=[jax.ShapeDtypeStruct(x.shape, x.dtype) for x in (queries, out_grad)],
        scratch_shapes=[pltpu.SemaphoreType.DMA((2,))],
        compiler_params=params(8),
        name="load",
    )(pinned(queries), pinned(out_grad))


def pack_kernel(q_ref, own_ref, other_ref, left_ref, right_ref, across_ref):
    width = q_ref.shape[1]
    odd = lax.axis_index("seq") % 2
    core = lax.axis_index("tp")
    cols = pl.ds(pl.multiple_of(core * width, HD), width)
    half = width // 2
    rows = pl.ds(pl.multiple_of((1 - odd) * BLK, BLK), BLK)
    left_ref[:BLK] = q_ref[rows, :half]
    right_ref[:BLK] = q_ref[rows, half:]
    across_ref[:BLK] = q_ref[pl.ds(pl.multiple_of(odd * BLK, BLK), BLK), :]
    lefts = pl.ds(pl.multiple_of(core * width, HD), half)
    rights = pl.ds(pl.multiple_of(core * width + half, HD), half)

    @pl.when(core != odd)
    def _():
        left_ref[BLK:] = own_ref[:, lefts]
        right_ref[BLK:] = own_ref[:, rights]
        across_ref[BLK:] = other_ref[:, cols]

    @pl.when(core == odd)
    def _():
        left_ref[BLK:] = other_ref[:, lefts]
        right_ref[BLK:] = other_ref[:, rights]
        across_ref[BLK:] = own_ref[:, cols]


def pack(queries, own, other):
    rows, width = queries.shape
    return pl.pallas_call(
        pack_kernel,
        in_specs=[WHOLE] * 3,
        out_specs=[WHOLE] * 3,
        out_shape=[jax.ShapeDtypeStruct((rows, cols), queries.dtype) for cols in (width // 2, width // 2, width)],
        compiler_params=params(8),
        name="pack",
    )(queries, own, other)


def stage_kernel(k_hbm, v_hbm, k_ref, v_ref, sems):
    rows = WIN // 4
    moves = []
    for i in range(4):
        part = pl.ds(i * rows, rows)
        moves.append(pltpu.make_async_copy(k_hbm.at[part, :], k_ref.at[part, :], sems.at[0, i]))
        moves.append(pltpu.make_async_copy(v_hbm.at[part, :], v_ref.at[part, :], sems.at[1, i]))
    for move in moves:
        move.start()
    for move in moves:
        move.wait()


def stage(keys, values):
    part = jax.ShapeDtypeStruct(keys.shape, keys.dtype)
    return pl.pallas_call(
        stage_kernel,
        in_specs=[RAW] * 2,
        out_specs=[WHOLE] * 2,
        out_shape=[part] * 2,
        scratch_shapes=[pltpu.SemaphoreType.DMA((2, 4))],
        compiler_params=params(16),
        cost_estimate=pl.CostEstimate(flops=0, bytes_accessed=8 * keys.size, transcendentals=0),
        name="stage",
    )(pinned(keys), pinned(values))


def at_end():
    index = lax.axis_index("seq")
    return (index == 0) | (index == lax.axis_size("seq") - 1)


def attend_left_kernel(m_ref, after_ref, k_ref, v_ref, gq_ref, p_ref, ds_ref):
    del after_ref
    attend_body(m_ref, k_ref, v_ref, gq_ref, p_ref, ds_ref, 0)


def attend_right_kernel(m_ref, left_ref, k_ref, v_ref, gq_ref, p_ref, ds_ref):
    start = left_ref.shape[1]
    gq_ref[:, :start] = left_ref[...]
    attend_body(m_ref, k_ref, v_ref, gq_ref.at[:, start:], p_ref, ds_ref, start)


def attend_across_kernel(own_ref, received_ref, k_ref, v_ref, gq_ref, p_ref, ds_ref, m_ref):
    @pl.when(at_end())
    def _():
        m_ref[...] = own_ref[...]

    @pl.when(jnp.logical_not(at_end()))
    def _():
        m_ref[...] = received_ref[...]

    attend_body(m_ref, k_ref, v_ref, gq_ref, p_ref, ds_ref, 0)


def attend_body(m_ref, k_ref, v_ref, gq_ref, p_ref, ds_ref, start):
    pairs = m_ref.shape[1] // PAIR
    held = {}

    def products(j):
        cols = pl.ds(j * PAIR, PAIR)
        window = pl.ds(start + j * PAIR, PAIR)
        scores = lax.dot_general(
            k_ref[:, window], diagonal(m_ref[:BLK, cols]), LAST, preferred_element_type=jnp.float32
        )
        dprobs = lax.dot_general(
            v_ref[:, window], diagonal(m_ref[BLK:, cols]), LAST, preferred_element_type=jnp.float32
        )
        held[j] = (scores, jnp.max(scores, axis=0, keepdims=True), dprobs)

    def sums(j):
        scores, top, dprobs = held[j]
        grown = jnp.exp2((scores - top) * (SCALE * LOG2E))
        inverse = 1.0 / jnp.sum(grown, axis=0, keepdims=True)
        delta = jnp.sum(grown * dprobs, axis=0, keepdims=True) * inverse
        held[j] = (grown, inverse, dprobs, delta)

    def results(j):
        grown, inverse, dprobs, delta = held.pop(j)
        cols = pl.ds(j * 2 * BLK, 2 * BLK)
        probs = grown * inverse
        p_ref[:, cols] = probs.astype(jnp.bfloat16)
        dscores = (probs * ((dprobs - delta) * SCALE)).astype(jnp.bfloat16)
        ds_ref[:, cols] = dscores
        both = lax.dot_general(
            dscores, k_ref[:, pl.ds(start + j * PAIR, PAIR)], FIRST, preferred_element_type=jnp.float32
        )
        gq_ref[:, pl.ds(j * PAIR, HD)] = both[:BLK, :HD].astype(jnp.bfloat16)
        gq_ref[:, pl.ds(j * PAIR + HD, HD)] = both[BLK:, HD:].astype(jnp.bfloat16)

    for step in range(pairs + 2):
        for stage_of, lag in ((products, 0), (sums, 1), (results, 2)):
            if 0 <= step - lag < pairs:
                stage_of(step - lag)


def after_kernel(array_ref, message_ref, out_ref):
    del message_ref
    out_ref[...] = array_ref[...]


def after(array, message):
    return pl.pallas_call(
        after_kernel,
        in_specs=[WHOLE] * 2,
        out_specs=WHOLE,
        out_shape=jax.ShapeDtypeStruct(array.shape, array.dtype),
        compiler_params=params(8),
        name="after",
    )(array, message)


def attend(kernel, message, others, keys, values, width, copied=None):
    heads = message.shape[1] // HD
    staged = jax.ShapeDtypeStruct((WIN, heads * BLK), jnp.bfloat16)
    shapes = [jax.ShapeDtypeStruct((BLK, width), jnp.bfloat16), staged, staged]
    if copied is not None:
        shapes.append(jax.ShapeDtypeStruct(copied.shape, copied.dtype))
    return pl.pallas_call(
        kernel,
        in_specs=[WHOLE] * (len(others) + 3),
        out_specs=[WHOLE] * len(shapes),
        out_shape=shapes,
        compiler_params=params(32),
        cost_estimate=pl.CostEstimate(
            flops=8 * BLK * WIN * HD * heads, bytes_accessed=6 * WIN * HD * heads, transcendentals=BLK * WIN * heads
        ),
        name="attend",
    )(message, *others, keys, values)


def event_kernel(pl_ref, dsl_ref, ml_ref, pr_ref, dsr_ref, mr_ref, p1_ref, ds1_ref, m1_ref, gk_hbm, gv_hbm, gk_ref, gv_ref, sems):
    parts = sems.shape[1]
    rows = WIN // parts
    moves = []
    pairs = gk_ref.shape[1] // PAIR
    half = pairs // 2
    for out, (left_ref, right_ref, a1, held, hbm, low) in enumerate(
        ((dsl_ref, dsr_ref, ds1_ref, gk_ref, gk_hbm, 0), (pl_ref, pr_ref, p1_ref, gv_ref, gv_hbm, BLK))
    ):
        block = pl.ds(low, BLK)
        rights = []
        for j in range(pairs):
            inside = (ml_ref if j < half else mr_ref)[block, pl.ds(j % half * PAIR, PAIR)]
            across = m1_ref[block, pl.ds(j * PAIR, PAIR)]
            rights.append(jnp.concatenate([diagonal(inside), diagonal(across)], axis=0))
        for part in range(parts):
            here = pl.ds(part * rows, rows)
            for j, right in enumerate(rights):
                inside = (left_ref if j < half else right_ref)[here, pl.ds(j % half * 2 * BLK, 2 * BLK)]
                left = jnp.concatenate([inside, a1[here, pl.ds(j * 2 * BLK, 2 * BLK)]], axis=1)
                held[here, pl.ds(j * PAIR, PAIR)] = jnp.dot(
                    left, right, preferred_element_type=jnp.float32
                ).astype(jnp.bfloat16)
            move = pltpu.make_async_copy(held.at[here, :], hbm.at[here, :], sems.at[out, part])
            move.start()
            moves.append(move)
    for move in moves:
        move.wait()


def event_grads(*args):
    width = args[-1].shape[1]
    out = jax.ShapeDtypeStruct((WIN, width), jnp.bfloat16)
    return pl.pallas_call(
        event_kernel,
        in_specs=[WHOLE] * 9,
        out_specs=[RAW] * 2,
        out_shape=[out] * 2,
        scratch_shapes=[pltpu.VMEM((WIN, width), jnp.bfloat16)] * 2 + [pltpu.SemaphoreType.DMA((2, 4))],
        compiler_params=params(32),
        cost_estimate=pl.CostEstimate(
            flops=8 * BLK * WIN * width, bytes_accessed=8 * WIN * width, transcendentals=0
        ),
        name="event_grads",
    )(*args)


def join_across_kernel(across_ref, own_ref, out_hbm, sem):
    odd = lax.axis_index("seq") % 2
    rows = out_hbm.at[pl.ds(pl.multiple_of(odd * BLK, BLK), BLK), :]

    @pl.when(at_end())
    def _():
        pltpu.make_async_copy(own_ref, rows, sem).start()

    @pl.when(jnp.logical_not(at_end()))
    def _():
        pltpu.make_async_copy(across_ref, rows, sem).start()

    pltpu.make_async_copy(across_ref, rows, sem).wait()


def join_inside_kernel(inside_ref, half_hbm, out_hbm, sem):
    odd = lax.axis_index("seq") % 2
    move = pltpu.make_async_copy(
        inside_ref, out_hbm.at[pl.ds(pl.multiple_of((1 - odd) * BLK, BLK), BLK), :], sem
    )
    move.start()
    move.wait()


def join_across(back_across, own_across):
    width = back_across.shape[1]
    return pl.pallas_call(
        join_across_kernel,
        in_specs=[WHOLE] * 2,
        out_specs=RAW,
        out_shape=jax.ShapeDtypeStruct((2 * BLK, width), back_across.dtype),
        scratch_shapes=[pltpu.SemaphoreType.DMA],
        compiler_params=params(8),
        name="join_across",
    )(back_across, own_across)


def join_inside(back_inside, half):
    return pl.pallas_call(
        join_inside_kernel,
        in_specs=[WHOLE, RAW],
        out_specs=RAW,
        out_shape=jax.ShapeDtypeStruct(half.shape, half.dtype),
        scratch_shapes=[pltpu.SemaphoreType.DMA],
        input_output_aliases={1: 0},
        compiler_params=params(8),
        name="join_inside",
    )(back_inside, half)


def shards(queries, keys, values, out_grad, starts):
    del starts
    seq = lax.axis_size("seq")
    frames, width = queries.shape
    assert frames == 2 * BLK and keys.shape[0] == WIN and seq % 2 == 0 and lax.axis_size("tp") == 2
    inside = [(i, i ^ 1) for i in range(seq)]
    across = [(0, 1), (1, 0), (2 * seq - 2, 2 * seq - 1), (2 * seq - 1, 2 * seq - 2)]
    for i in range(1, seq - 1):
        partner = i + 1 if i % 2 else i - 1
        across += [(2 * i + core, 2 * partner + core) for core in range(2)]

    other = lax.ppermute(out_grad, "tp", [(0, 1), (1, 0)])
    left, right, second = pack(*load(queries, out_grad), other)
    got_second = lax.ppermute(second, ("seq", "tp"), across)
    got_left = lax.ppermute(left, "seq", inside)
    got_right = lax.ppermute(right, "seq", inside)
    keys, values = stage(keys, values)
    gq1, p1, ds1, used = attend(attend_across_kernel, second, [got_second], keys, values, width, second)
    sent = after(gq1, got_left)
    back1 = lax.ppermute(sent, ("seq", "tp"), across)
    gql, *lefts = attend(attend_left_kernel, got_left, [sent], keys, values, width // 2)
    gq0, *rights = attend(attend_right_kernel, got_right, [gql], keys, values, width)
    back0 = lax.ppermute(gq0, "seq", inside)
    grad_keys, grad_values = event_grads(*lefts, got_left, *rights, got_right, p1, ds1, used)
    return join_inside(back0, join_across(back1, gq1)), grad_keys, grad_values


def solution(mesh):
    return jax.shard_map(
        shards,
        mesh=mesh,
        in_specs=(
            P(("group", "seq"), "tp"),
            P(("group", "seq"), "tp"),
            P(("group", "seq"), "tp"),
            P(("group", "seq", "tp"), None),
            P("group"),
        ),
        out_specs=(P(("group", "seq"), "tp"), P(("group", "seq"), "tp"), P(("group", "seq"), "tp")),
        check_vma=False,
    )
```
